512 devices in a mesh: dp: 16 (over x, z_hi), ctx: 32 (over z_lo, y, core).
Axes of the slice: x: 4, y: 8, z: 8 (z_hi: 4, z_lo: 2; z = z_hi * 2 + z_lo), core: 2. Of those that a mesh axis runs over, the one named last changes fastest.
Arguments:
- act_input: bfloat16 [81920, 2048], P(('dp', 'ctx')), may hold values from -150 to 150
- out_grad: bfloat16 [81920, 2048], P(('dp', 'ctx')), may hold values from -150 to 150
Outputs:
- act_factor: float32 [32, 16, 16, 512], P('ctx', 'dp')
- grad_factor: float32 [32, 16, 16, 512], P('ctx', 'dp')
The draws below stay inside these ranges and needn't reach their ends.
All inputs are finite; a program needn't handle non-finite values.
Results may differ from the reference program's by a relative error of at most 0.0003.
Values may be sent and summed in bfloat16 or wider, within the bound.
A program may use at most 64 MiB of HBM per device.

```python
import jax
import jax.numpy as jnp
from jax import lax

W = 2048
TOKENS = 81920
GRID_R = 2
GRID_C = 4
TILE_R = 1024
TILE_C = 512
PIECE = 16
N_DP = 16
N_CTX = 32


def stream_scales(key):
    subkeys = jax.random.split(jax.random.fold_in(key, 5), 2)
    depth = jax.random.uniform(subkeys[0], (), dtype=jnp.float32, minval=0.35, maxval=0.6)
    flipped = jax.random.uniform(subkeys[1], (), dtype=jnp.float32) < 0.5
    shrink = 10.0 ** (-depth)
    act_scale = jnp.where(flipped, shrink, 1.0)
    grad_scale = jnp.where(flipped, 1.0, shrink)
    return (act_scale, grad_scale)


def draw_tokens(key, stream_tag, rising, stream_scale):
    subkeys = jax.random.split(jax.random.fold_in(key, stream_tag), 5)
    row_pos = jnp.arange(TOKENS, dtype=jnp.float32) / TOKENS
    feat_ids = jnp.arange(W, dtype=jnp.int32)
    owner_group = feat_ids % TILE_R % (TILE_R // 4) // PIECE
    group_frac = owner_group.astype(jnp.float32) / max(N_DP - 1, 1)
    if not rising:
        group_frac = 1.0 - group_frac
    group_power = 0.5
    trend_up = rising
    if trend_up:
        trend_pos = row_pos
    else:
        trend_pos = 1.0 - row_pos
    feat_scale = 10.0 ** (group_power * group_frac + 0.2 * jax.random.uniform(subkeys[0], (W,), dtype=jnp.float32))
    block_ids = jnp.arange(TOKENS, dtype=jnp.int32) * 64 // TOKENS
    block_table = 10.0 ** (0.3 * jax.random.uniform(subkeys[4], (64,), dtype=jnp.float32))
    block_scale = block_table[block_ids]
    row_scale = 3.0 ** (0.5 * trend_pos) * block_scale * 10.0 ** (0.15 * jax.random.uniform(subkeys[1], (TOKENS,), dtype=jnp.float32))
    raw_values = jnp.clip(jax.random.normal(subkeys[3], (TOKENS, W), dtype=jnp.float32), -5.0, 5.0)
    return raw_values * (stream_scale * row_scale)[:, None] * feat_scale[None, :]


def draw_act_input(key, part):
    act_scale, grad_scale = stream_scales(key)
    return draw_tokens(key, 11, True, act_scale).astype(jnp.bfloat16)


def draw_out_grad(key, part):
    act_scale, grad_scale = stream_scales(key)
    return draw_tokens(key, 23, False, grad_scale).astype(jnp.bfloat16)


def setup_inputs(seed: int = 0) -> dict:
    key_list = jax.random.split(jax.random.key(seed), 3)
    act_input = draw_act_input(jax.random.fold_in(key_list[2], 71), 0)
    out_grad = draw_out_grad(jax.random.fold_in(key_list[2], 71), 0)
    return {"act_input": act_input, "out_grad": out_grad}


damping = 1.0

def covariance(samples):
    wide = samples.astype(jnp.float32)
    return jnp.dot(wide.T, wide, precision=lax.Precision.HIGHEST) / TOKENS

def tiles_of(full):
    blocks = full.reshape(GRID_R, TILE_R, GRID_C, TILE_C).transpose(0, 2, 1, 3)
    return blocks.reshape(N_CTX, N_DP, PIECE, TILE_C)

def reference(act_input, out_grad):
    act_cov = covariance(act_input)
    grad_cov = covariance(out_grad)
    ratio = jnp.sqrt(jnp.trace(act_cov) / jnp.trace(grad_cov))
    identity = jnp.eye(W, dtype=jnp.float32)
    act_damped = act_cov + ratio * damping * identity
    grad_damped = grad_cov + damping / ratio * identity
    return (tiles_of(act_damped), tiles_of(grad_damped))
```

```python
import jax
import jax.numpy as jnp
from jax import lax
from jax.experimental import pallas as pl
from jax.experimental.pallas import tpu as pltpu
from jax.sharding import PartitionSpec as P

damping = 1.0

NX, NY, NZ = 4, 8, 8
ROWS = 160
HALF = ROWS // 2
W = 2048
HW = W // 2
BLK = 128
NB = HW // BLK
TOKENS = ROWS * 2 * NX * NY * NZ
MESH = pl.DeviceIdType.MESH

STREAMS = ((0, 1, 4), (0, -1, 3), (1, 1, 3), (1, -1, 4))
BASE = (0, 4, 7, 10)
NSLOT = 14


def device(x, y, z, c):
    return (x * (NZ // 2) + z // 2, (z % 2) * (2 * NY) + y * 2 + c)


def kernel(act, grad, act_out, grad_out,
           xb, pk, r1, r2, outbox, inbox, dg, gy, gz, gx, gc,
           loc_sem, raw_s, raw_r, s1_s, s1_r, s2_s, s2_r,
           dg_s, dg_r, out_s, out_r):
    dp = lax.axis_index("dp")
    ctx = lax.axis_index("ctx")
    x = dp // (NZ // 2)
    z = (dp % (NZ // 2)) * 2 + ctx // (2 * NY)
    y = (ctx // 2) % NY
    c = ctx % 2
    par = x % 2

    def at_x(d):
        return device((x + d) % NX, y, z, c)

    def at_y(d):
        return device(x, (y + d) % NY, z, c)

    def at_z(d):
        return device(x, y, (z + d) % NZ, c)

    partner = device(x, y, z, 1 - c)

    def remote(src, dst, ssem, rsem, dev):
        return pltpu.make_async_remote_copy(
            src_ref=src, dst_ref=dst, send_sem=ssem, recv_sem=rsem,
            device_id=dev, device_id_type=MESH)

    barrier = pltpu.get_barrier_semaphore()
    peers = [partner] + [at_x(d) for d in range(1, NX)]
    peers += [at_y(d) for d in range(1, NY)] + [at_z(d) for d in range(1, NZ)]
    for dev in peers:
        pl.semaphore_signal(barrier, inc=1, device_id=dev, device_id_type=MESH)

    own_rows = xb.at[pl.ds(0, ROWS)]

    @pl.when(par == 0)
    def _():
        pltpu.make_async_copy(act, own_rows, loc_sem).start()

    @pl.when(par == 1)
    def _():
        pltpu.make_async_copy(grad, own_rows, loc_sem).start()

    pl.semaphore_wait(barrier, len(peers))

    def raw_copies(own, other):
        copies = []
        for h in range(2):
            cols = pl.ds(h * HW, HW)
            copies.append(remote(
                other.at[pl.ds(0, HALF), cols],
                xb.at[pl.ds(2 * ROWS, HALF), cols],
                raw_s.at[2 * h], raw_r.at[2 * h], at_x(1)))
            copies.append(remote(
                other.at[pl.ds(HALF, HALF), cols],
                xb.at[pl.ds(2 * ROWS + HALF, HALF), cols],
                raw_s.at[2 * h + 1], raw_r.at[2 * h + 1], at_x(-1)))
        copies.append(remote(own, xb.at[pl.ds(ROWS, ROWS)],
                             raw_s.at[4], raw_r.at[4], partner))
        return copies

    @pl.when(par == 0)
    def _():
        for copy in raw_copies(act, grad):
            copy.start()

    @pl.when(par == 1)
    def _():
        for copy in raw_copies(grad, act):
            copy.start()

    raw = raw_copies(act, grad)
    pltpu.make_async_copy(act, own_rows, loc_sem).wait()
    raw[4].wait_recv()

    contract = (((0,), (0,)), ((), ()))

    def gram(row, lo, ro):
        left = xb[pl.ds(row, 2 * ROWS), pl.ds(pl.multiple_of(lo, 256), 256)]
        right = xb[pl.ds(row, 2 * ROWS), pl.ds(pl.multiple_of(ro, 256), 256)]
        return lax.dot_general(left, right, contract,
                               preferred_element_type=jnp.float32)

    upper = (lax.broadcasted_iota(jnp.int32, (256, 256), 0)
             < lax.broadcasted_iota(jnp.int32, (256, 256), 1))

    def store(a, b, value, add):
        for i in range(2):
            for j in range(2):
                part = value[BLK * i:BLK * (i + 1), BLK * j:BLK * (j + 1)]
                if add:
                    part = part + pk[2 * a + i, 2 * b + j]
                pk[2 * a + i, 2 * b + j] = part

    def diagonal_blocks(row, add):
        def step(a, carry):
            first = gram(row, 256 * a, 256 * a)
            second = gram(row, HW + 256 * a, HW + 256 * a)
            store(a, a, jnp.where(upper, first, second), add)
            return carry
        lax.fori_loop(0, 4, step, 0)

    def tile_grid(row, add):
        def step(a, carry):
            for b in range(4):
                low = jnp.where(a > b, HW, 0)
                lo = 256 * a + jnp.where(c == 0, 0, low)
                ro = 256 * b + jnp.where(c == 0, HW, low)
                value = gram(row, lo, ro)

                @pl.when(jnp.logical_or(c == 0, a != b))
                def _():
                    store(a, b, value, add)
            return carry
        lax.fori_loop(0, 4, step, 0)

        @pl.when(c == 1)
        def _():
            diagonal_blocks(row, add)

    tile_grid(0, False)

    relay = []
    for h in range(2):
        for s in range(2):
            raw[2 * h + s].wait_recv()
            rows = pl.ds(2 * ROWS + HALF * s, HALF)
            to = pl.ds(3 * ROWS + HALF * s, HALF)
            cols = pl.ds(h * HW, HW)
            copy = remote(xb.at[rows, cols], xb.at[to, cols],
                          raw_s.at[5 + 2 * h + s], raw_r.at[5 + 2 * h + s], partner)
            copy.start()
            relay.append(copy)
    for copy in relay:
        copy.wait_recv()

    tile_grid(2 * ROWS, True)

    def chunk1(k, o, h):
        if k == 0:
            return pk.at[o, pl.ds(4 * h, 4), pl.ds(0, 64), :]
        return pk.at[pl.ds(4 * h, 4), o, pl.ds(64, 64), :]

    def chunk2(k, o, h):
        if k == 0:
            return pk.at[y, o, pl.ds(32 * h, 32), :]
        return pk.at[o, z, pl.ds(64 + 32 * h, 32), :]

    def ring(chunk, slots, ssem, rsem, axes, between):
        copies = {}
        for t in range(5):
            for i, (h, sign, hops) in enumerate(STREAMS):
                if t > hops:
                    continue
                for k in range(2):
                    pos, at = axes[k]
                    n = NY
                    o = (pos + sign * (hops - t)) % n
                    ref = chunk(k, o, h)
                    if t > 0:
                        copies[k, i, t - 1].wait_recv()
                        ref[...] = ref[...] + slots[k * NSLOT + BASE[i] + t - 1]
                    if t < hops:
                        slot = k * NSLOT + BASE[i] + t
                        copy = remote(ref, slots.at[slot], ssem.at[slot],
                                      rsem.at[slot], at(sign))
                        copy.start()
                        copies[k, i, t] = copy
            between(t)
        return copies

    diag_copies = []

    def diag_send(srcs, dsts, devs, base):
        copies = []
        for n, (src, dst, dev) in enumerate(zip(srcs, dsts, devs)):
            copy = remote(src, dst, dg_s.at[base + n], dg_r.at[base + n], dev)
            copy.start()
            copies.append(copy)
        diag_copies.extend(copies)
        return copies

    pending = {}

    def between1(t):
        if t == 0:
            for i in range(NB):
                cols = pl.ds(pl.multiple_of(c * HW + BLK * i, BLK), BLK)
                part = xb[:, cols].astype(jnp.float32)
                dg[0, pl.ds(i, 1), :] = jnp.sum(part * part, axis=0, keepdims=True)
            pending["y"] = diag_send(
                [dg.at[0]] * 7, [gy.at[d - 1] for d in range(1, NY)],
                [at_y(d) for d in range(1, NY)], 0)
        elif t == 1:
            total = dg[0]
            for d in range(7):
                pending["y"][d].wait_recv()
                total = total + gy[d]
            dg[1] = total
            pending["z"] = diag_send(
                [dg.at[1]] * 7, [gz.at[d - 1] for d in range(1, NZ)],
                [at_z(d) for d in range(1, NZ)], 7)
        elif t == 2:
            total = dg[1]
            for d in range(7):
                pending["z"][d].wait_recv()
                total = total + gz[d]
            gx[x] = total
            pending["x"] = diag_send(
                [gx.at[x]] * 3, [gx.at[x]] * 3,
                [at_x(d) for d in range(1, NX)], 14)
        elif t == 3:
            for d in range(1, NX):
                src = (x - d) % NX
                remote(gx.at[src], gx.at[src], dg_s.at[13 + d], dg_r.at[13 + d],
                       at_x(d)).wait_recv()
            pending["c"] = diag_send([gx], [gc], [partner], 17)
        else:
            pending["c"][0].wait_recv()

    first = ring(chunk1, r1, s1_s, s1_r, ((y, at_y), (z, at_z)), between1)
    second = ring(chunk2, r2, s2_s, s2_r, ((z, at_z), (y, at_y)), lambda t: None)

    piece = pk[y, z]
    flipped = piece.T
    below = (lax.broadcasted_iota(jnp.int32, (BLK, BLK), 0)
             > lax.broadcasted_iota(jnp.int32, (BLK, BLK), 1))
    packed = jnp.logical_and(c == 1, y == z)
    swap = jnp.logical_and(below, packed)
    outbox[0] = jnp.where(swap, flipped, piece)
    outbox[1] = jnp.where(swap, piece, flipped)

    off_a = jnp.where(y > z, NB, 0)
    off_b = jnp.where(y >= z, NB, 0)
    blocks = (
        (y + jnp.where(c == 0, 0, off_a), z + jnp.where(c == 0, NB, off_a)),
        (z + jnp.where(c == 0, NB, off_b), y + jnp.where(c == 0, 0, off_b)),
    )
    me = (dp, ctx)
    sends = []
    for g in range(2):
        bi, bj = blocks[g]
        slot = par * 8 + (x // 2) * 4 + bj % 4
        for s in range(8):
            dev = device(2 * (bi % 2) + s // 4, 2 * (bj // 4) + (bi // 4) % 2,
                         2 * (s % 4) + bi // 8, (bi // 2) % 2)
            is_me = jnp.logical_and(dev[0] == me[0], dev[1] == me[1])
            src = outbox.at[g, pl.ds(16 * s, 16), :]
            dst = inbox.at[slot]
            copy = remote(src, dst, out_s.at[8 * g + s], out_r.at[slot], dev)

            @pl.when(is_me)
            def _():
                pltpu.make_async_copy(src, dst, out_r.at[slot]).start()

            @pl.when(jnp.logical_not(is_me))
            def _():
                copy.start()
            sends.append((copy, is_me))

    mine = [gx[n] for n in range(NX)]
    theirs = [gc[n] for n in range(NX)]
    diag = [(mine[f] + mine[f + 2], theirs[f] + theirs[f + 2]) for f in range(2)]
    row_block = (z % 2) * 8 + (y % 2) * 4 + c * 2 + x // 2
    strip = (x % 2) * 4 + z // 2
    own_half = (row_block // 8) == c
    pick = lax.broadcasted_iota(jnp.int32, (8, BLK), 0) == row_block % 8
    trace = []
    values = []
    for a, b in diag:
        trace.append(jnp.sum(a + b, keepdims=True))
        chosen = jnp.where(own_half, a, b)
        values.append(jnp.sum(jnp.where(pick, chosen, 0.0), axis=0, keepdims=True))
    ratio = jnp.sqrt(trace[0] / trace[1])
    shift = (ratio * damping, damping / ratio)
    scale = 1.0 / TOKENS
    on_diag = (lax.broadcasted_iota(jnp.int32, (16, BLK), 1)
               == lax.broadcasted_iota(jnp.int32, (16, BLK), 0) + 16 * strip)
    for f in range(2):
        out = (act_out, grad_out)[f]
        damped = values[f] * scale + shift[f]
        for j in range(4):
            for n in range(2):
                slot = 8 * f + 4 * n + j
                pltpu.make_async_copy(outbox.at[0, pl.ds(0, 16), :], inbox.at[slot],
                                      out_r.at[slot]).wait()
            here = jnp.logical_and(on_diag, (y // 2) * 4 + j == row_block)
            value = (inbox[8 * f + j] + inbox[8 * f + 4 + j]) * scale
            out[:, BLK * j:BLK * (j + 1)] = jnp.where(here, damped, value)

    for copy, is_me in sends:
        @pl.when(jnp.logical_not(is_me))
        def _():
            copy.wait_send()
    for copy in raw + relay + list(first.values()) + list(second.values()) + diag_copies:
        copy.wait_send()


def on_device(act_input, out_grad):
    f32 = jnp.float32
    piece = jax.ShapeDtypeStruct((16, 4 * BLK), f32)
    any_space = pl.BlockSpec(memory_space=pl.ANY)
    vmem = pl.BlockSpec(memory_space=pltpu.VMEM)
    dma = pltpu.SemaphoreType.DMA
    act_out, grad_out = pl.pallas_call(
        kernel,
        out_shape=(piece, piece),
        in_specs=[any_space, any_space],
        out_specs=(vmem, vmem),
        scratch_shapes=[
            pltpu.VMEM((4 * ROWS, W), jnp.bfloat16),
            pltpu.VMEM((NB, NB, BLK, BLK), f32),
            pltpu.VMEM((2 * NSLOT, 4, 64, BLK), f32),
            pltpu.VMEM((2 * NSLOT, 32, BLK), f32),
            pltpu.VMEM((2, BLK, BLK), f32),
            pltpu.VMEM((16, 16, BLK), f32),
            pltpu.VMEM((2, 8, BLK), f32),
            pltpu.VMEM((7, 8, BLK), f32),
            pltpu.VMEM((7, 8, BLK), f32),
            pltpu.VMEM((NX, 8, BLK), f32),
            pltpu.VMEM((NX, 8, BLK), f32),
            dma,
            dma((9,)), dma((9,)),
            dma((2 * NSLOT,)), dma((2 * NSLOT,)),
            dma((2 * NSLOT,)), dma((2 * NSLOT,)),
            dma((18,)), dma((18,)),
            dma((16,)), dma((16,)),
        ],
        compiler_params=pltpu.CompilerParams(
            collective_id=0, has_side_effects=True,
            vmem_limit_bytes=48 * 1024 * 1024),
        name="kfac",
    )(act_input, out_grad)
    return act_out[None, None], grad_out[None, None]


def solution(mesh):
    placed = (P(("dp", "ctx"), None), P(("dp", "ctx"), None))
    return jax.shard_map(
        on_device,
        mesh=mesh,
        in_specs=placed,
        out_specs=(P("ctx", "dp", None, None), P("ctx", "dp", None, None)),
        check_vma=False,
    )
```

```python
import jax
import jax.numpy as jnp
from jax import lax
from jax.experimental import pallas as pl
from jax.experimental.pallas import tpu as pltpu
from jax.sharding import PartitionSpec as P

damping = 1.0

NX, NY, NZ = 4, 8, 8
ROWS = 160
HALF = ROWS // 2
W = 2048
HW = W // 2
BLK = 128
NB = HW // BLK
TOKENS = ROWS * 2 * NX * NY * NZ
MESH = pl.DeviceIdType.MESH

STREAMS = ((0, 1, 4), (0, -1, 3), (1, 1, 3), (1, -1, 4))
BASE = (0, 4, 7, 10)
NSLOT = 14


def device(x, y, z, c):
    return (x * (NZ // 2) + z // 2, (z % 2) * (2 * NY) + y * 2 + c)


def kernel(act, grad, act_out, grad_out,
           xb, pk, r1, r2, outbox, inbox, dg, gy, gz, gx, gc,
           loc_sem, raw_s, raw_r, s1_s, s1_r, s2_s, s2_r,
           dg_s, dg_r, out_s, out_r):
    dp = lax.axis_index("dp")
    ctx = lax.axis_index("ctx")
    x = dp // (NZ // 2)
    z = (dp % (NZ // 2)) * 2 + ctx // (2 * NY)
    y = (ctx // 2) % NY
    c = ctx % 2
    par = x % 2

    def at_x(d):
        return device((x + d) % NX, y, z, c)

    def at_y(d):
        return device(x, (y + d) % NY, z, c)

    def at_z(d):
        return device(x, y, (z + d) % NZ, c)

    partner = device(x, y, z, 1 - c)

    def remote(src, dst, ssem, rsem, dev):
        return pltpu.make_async_remote_copy(
            src_ref=src, dst_ref=dst, send_sem=ssem, recv_sem=rsem,
            device_id=dev, device_id_type=MESH)

    barrier = pltpu.get_barrier_semaphore()
    peers = [partner] + [at_x(d) for d in range(1, NX)]
    peers += [at_y(d) for d in range(1, NY)] + [at_z(d) for d in range(1, NZ)]
    for dev in peers:
        pl.semaphore_signal(barrier, inc=1, device_id=dev, device_id_type=MESH)

    own_rows = xb.at[pl.ds(0, ROWS)]

    @pl.when(par == 0)
    def _():
        pltpu.make_async_copy(act, own_rows, loc_sem).start()

    @pl.when(par == 1)
    def _():
        pltpu.make_async_copy(grad, own_rows, loc_sem).start()

    pl.semaphore_wait(barrier, len(peers))

    def raw_copies(own, other):
        copies = []
        for h in range(2):
            cols = pl.ds(h * HW, HW)
            copies.append(remote(
                other.at[pl.ds(0, HALF), cols],
                xb.at[pl.ds(2 * ROWS, HALF), cols],
                raw_s.at[2 * h], raw_r.at[2 * h], at_x(1)))
            copies.append(remote(
                other.at[pl.ds(HALF, HALF), cols],
                xb.at[pl.ds(2 * ROWS + HALF, HALF), cols],
                raw_s.at[2 * h + 1], raw_r.at[2 * h + 1], at_x(-1)))
        copies.append(remote(own, xb.at[pl.ds(ROWS, ROWS)],
                             raw_s.at[4], raw_r.at[4], partner))
        return copies

    @pl.when(par == 0)
    def _():
        for copy in raw_copies(act, grad):
            copy.start()

    @pl.when(par == 1)
    def _():
        for copy in raw_copies(grad, act):
            copy.start()

    raw = raw_copies(act, grad)
    pltpu.make_async_copy(act, own_rows, loc_sem).wait()
    raw[4].wait_recv()

    contract = (((0,), (0,)), ((), ()))

    def product(rows, left, right):
        return lax.dot_general(xb[rows, left], xb[rows, right], contract,
                               preferred_element_type=jnp.float32)

    upper = (lax.broadcasted_iota(jnp.int32, (256, 256), 0)
             < lax.broadcasted_iota(jnp.int32, (256, 256), 1))

    def store(a, b, value, add):
        for i in range(2):
            for j in range(2):
                part = value[BLK * i:BLK * (i + 1), BLK * j:BLK * (j + 1)]
                if add:
                    part = part + pk[2 * a + i, 2 * b + j]
                pk[2 * a + i, 2 * b + j] = part

    def tile_grid(row, add):
        rows = pl.ds(row, 2 * ROWS)

        @pl.when(c == 0)
        def _():
            for a in range(4):
                value = product(rows, pl.ds(256 * a, 256), pl.ds(HW, HW))
                for b in range(4):
                    store(a, b, value[:, 256 * b:256 * (b + 1)], add)

        @pl.when(c == 1)
        def _():
            for a in range(4):
                first = product(rows, pl.ds(256 * a, 256), pl.ds(256 * a, HW - 256 * a))
                second = product(rows, pl.ds(HW + 256 * a, 256), pl.ds(HW, 256 * (a + 1)))
                for b in range(4):
                    high = first[:, 256 * (b - a):256 * (b - a + 1)] if b >= a else None
                    low = second[:, 256 * b:256 * (b + 1)] if b <= a else None
                    if high is None:
                        store(a, b, low, add)
                    elif low is None:
                        store(a, b, high, add)
                    else:
                        store(a, b, jnp.where(upper, high, low), add)

    tile_grid(0, False)

    relay = []
    for h in range(2):
        for s in range(2):
            raw[2 * h + s].wait_recv()
            rows = pl.ds(2 * ROWS + HALF * s, HALF)
            to = pl.ds(3 * ROWS + HALF * s, HALF)
            cols = pl.ds(h * HW, HW)
            copy = remote(xb.at[rows, cols], xb.at[to, cols],
                          raw_s.at[5 + 2 * h + s], raw_r.at[5 + 2 * h + s], partner)
            copy.start()
            relay.append(copy)
    for copy in relay:
        copy.wait_recv()

    tile_grid(2 * ROWS, True)

    def chunk1(k, o, h):
        if k == 0:
            return pk.at[o, pl.ds(4 * h, 4), pl.ds(0, 64), :]
        return pk.at[pl.ds(4 * h, 4), o, pl.ds(64, 64), :]

    def ring(chunk, slots, ssem, rsem, axes, between):
        copies = {}
        for t in range(5):
            for i, (h, sign, hops) in enumerate(STREAMS):
                if t > hops:
                    continue
                for k in range(2):
                    pos, at = axes[k]
                    n = NY
                    o = (pos + sign * (hops - t)) % n
                    ref = chunk(k, o, h)
                    if t > 0:
                        copies[k, i, t - 1].wait_recv()
                        ref[...] = ref[...] + slots[k * NSLOT + BASE[i] + t - 1]
                    if t < hops:
                        slot = k * NSLOT + BASE[i] + t
                        copy = remote(ref, slots.at[slot], ssem.at[slot],
                                      rsem.at[slot], at(sign))
                        copy.start()
                        copies[k, i, t] = copy
            between(t)
        return copies

    diag_copies = []

    def diag_send(srcs, dsts, devs, base):
        copies = []
        for n, (src, dst, dev) in enumerate(zip(srcs, dsts, devs)):
            copy = remote(src, dst, dg_s.at[base + n], dg_r.at[base + n], dev)
            copy.start()
            copies.append(copy)
        diag_copies.extend(copies)
        return copies

    pending = {}

    def between1(t):
        if t == 0:
            for i in range(NB):
                cols = pl.ds(pl.multiple_of(c * HW + BLK * i, BLK), BLK)
                part = xb[:, cols].astype(jnp.float32)
                dg[0, pl.ds(i, 1), :] = jnp.sum(part * part, axis=0, keepdims=True)
            pending["y"] = diag_send(
                [dg.at[0]] * 7, [gy.at[d - 1] for d in range(1, NY)],
                [at_y(d) for d in range(1, NY)], 0)
        elif t == 1:
            total = dg[0]
            for d in range(7):
                pending["y"][d].wait_recv()
                total = total + gy[d]
            dg[1] = total
            pending["z"] = diag_send(
                [dg.at[1]] * 7, [gz.at[d - 1] for d in range(1, NZ)],
                [at_z(d) for d in range(1, NZ)], 7)
        elif t == 2:
            total = dg[1]
            for d in range(7):
                pending["z"][d].wait_recv()
                total = total + gz[d]
            gx[x] = total
            pending["x"] = diag_send(
                [gx.at[x]] * 3, [gx.at[x]] * 3,
                [at_x(d) for d in range(1, NX)], 14)
        elif t == 3:
            for d in range(1, NX):
                src = (x - d) % NX
                remote(gx.at[src], gx.at[src], dg_s.at[13 + d], dg_r.at[13 + d],
                       at_x(d)).wait_recv()
            pending["c"] = diag_send([gx], [gc], [partner], 17)
        else:
            pending["c"][0].wait_recv()

    first = ring(chunk1, r1, s1_s, s1_r, ((y, at_y), (z, at_z)), between1)
    second = []
    for d in (4, 3, 5, 2, 6, 1, 7):
        for k in range(2):
            if k == 0:
                src, dev = pk.at[y, (z + d) % NZ, pl.ds(0, 64), :], at_z(d)
            else:
                src, dev = pk.at[(y + d) % NY, z, pl.ds(64, 64), :], at_y(d)
            slot = 7 * k + d - 1
            copy = remote(src, r2.at[slot], s2_s.at[slot], s2_r.at[slot], dev)
            copy.start()
            second.append((k, slot, copy))
    sums = [pk[y, z, pl.ds(0, 64), :], pk[y, z, pl.ds(64, 64), :]]
    for k, slot, copy in sorted(second, key=lambda e: min(e[1] % 7, 6 - e[1] % 7)):
        copy.wait_recv()
        sums[k] = sums[k] + r2[slot]

    piece = jnp.concatenate(sums, axis=0)
    flipped = piece.T
    below = (lax.broadcasted_iota(jnp.int32, (BLK, BLK), 0)
             > lax.broadcasted_iota(jnp.int32, (BLK, BLK), 1))
    packed = jnp.logical_and(c == 1, y == z)
    swap = jnp.logical_and(below, packed)
    outbox[0] = jnp.where(swap, flipped, piece)
    outbox[1] = jnp.where(swap, piece, flipped)

    off_a = jnp.where(y > z, NB, 0)
    off_b = jnp.where(y >= z, NB, 0)
    blocks = (
        (y + jnp.where(c == 0, 0, off_a), z + jnp.where(c == 0, NB, off_a)),
        (z + jnp.where(c == 0, NB, off_b), y + jnp.where(c == 0, 0, off_b)),
    )
    me = (dp, ctx)
    sends = []
    for g in range(2):
        bi, bj = blocks[g]
        slot = par * 8 + (x // 2) * 4 + bj % 4
        for s in range(8):
            dev = device(2 * (bi % 2) + s // 4, 2 * (bj // 4) + (bi // 4) % 2,
                         2 * (s % 4) + bi // 8, (bi // 2) % 2)
            is_me = jnp.logical_and(dev[0] == me[0], dev[1] == me[1])
            src = outbox.at[g, pl.ds(16 * s, 16), :]
            dst = inbox.at[slot]
            copy = remote(src, dst, out_s.at[8 * g + s], out_r.at[slot], dev)

            @pl.when(is_me)
            def _():
                pltpu.make_async_copy(src, dst, out_r.at[slot]).start()

            @pl.when(jnp.logical_not(is_me))
            def _():
                copy.start()
            sends.append((copy, is_me))

    mine = [gx[n] for n in range(NX)]
    theirs = [gc[n] for n in range(NX)]
    diag = [(mine[f] + mine[f + 2], theirs[f] + theirs[f + 2]) for f in range(2)]
    row_block = (z % 2) * 8 + (y % 2) * 4 + c * 2 + x // 2
    strip = (x % 2) * 4 + z // 2
    own_half = (row_block // 8) == c
    pick = lax.broadcasted_iota(jnp.int32, (8, BLK), 0) == row_block % 8
    trace = []
    values = []
    for a, b in diag:
        trace.append(jnp.sum(a + b, keepdims=True))
        chosen = jnp.where(own_half, a, b)
        values.append(jnp.sum(jnp.where(pick, chosen, 0.0), axis=0, keepdims=True))
    ratio = jnp.sqrt(trace[0] / trace[1])
    shift = (ratio * damping, damping / ratio)
    scale = 1.0 / TOKENS
    on_diag = (lax.broadcasted_iota(jnp.int32, (16, BLK), 1)
               == lax.broadcasted_iota(jnp.int32, (16, BLK), 0) + 16 * strip)
    for f in range(2):
        out = (act_out, grad_out)[f]
        damped = values[f] * scale + shift[f]
        for j in range(4):
            for n in range(2):
                slot = 8 * f + 4 * n + j
                pltpu.make_async_copy(outbox.at[0, pl.ds(0, 16), :], inbox.at[slot],
                                      out_r.at[slot]).wait()
            here = jnp.logical_and(on_diag, (y // 2) * 4 + j == row_block)
            value = (inbox[8 * f + j] + inbox[8 * f + 4 + j]) * scale
            out[:, BLK * j:BLK * (j + 1)] = jnp.where(here, damped, value)

    for copy, is_me in sends:
        @pl.when(jnp.logical_not(is_me))
        def _():
            copy.wait_send()
    for copy in raw + relay + list(first.values()) + [copy for _, _, copy in second] + diag_copies:
        copy.wait_send()


def on_device(act_input, out_grad):
    f32 = jnp.float32
    piece = jax.ShapeDtypeStruct((16, 4 * BLK), f32)
    any_space = pl.BlockSpec(memory_space=pltpu.HBM)
    vmem = pl.BlockSpec(memory_space=pltpu.VMEM)
    dma = pltpu.SemaphoreType.DMA
    act_out, grad_out = pl.pallas_call(
        kernel,
        out_shape=(piece, piece),
        in_specs=[any_space, any_space],
        out_specs=(vmem, vmem),
        scratch_shapes=[
            pltpu.VMEM((4 * ROWS, W), jnp.bfloat16),
            pltpu.VMEM((NB, NB, BLK, BLK), f32),
            pltpu.VMEM((2 * NSLOT, 4, 64, BLK), f32),
            pltpu.VMEM((14, 64, BLK), f32),
            pltpu.VMEM((2, BLK, BLK), f32),
            pltpu.VMEM((16, 16, BLK), f32),
            pltpu.VMEM((2, 8, BLK), f32),
            pltpu.VMEM((7, 8, BLK), f32),
            pltpu.VMEM((7, 8, BLK), f32),
            pltpu.VMEM((NX, 8, BLK), f32),
            pltpu.VMEM((NX, 8, BLK), f32),
            dma,
            dma((9,)), dma((9,)),
            dma((2 * NSLOT,)), dma((2 * NSLOT,)),
            dma((2 * NSLOT,)), dma((2 * NSLOT,)),
            dma((18,)), dma((18,)),
            dma((16,)), dma((16,)),
        ],
        compiler_params=pltpu.CompilerParams(
            collective_id=0, has_side_effects=True,
            vmem_limit_bytes=62 * 1024 * 1024),
        name="kfac",
    )(act_input, out_grad)
    return act_out[None, None], grad_out[None, None]


def solution(mesh):
    placed = (P(("dp", "ctx"), None), P(("dp", "ctx"), None))
    return jax.shard_map(
        on_device,
        mesh=mesh,
        in_specs=placed,
        out_specs=(P("ctx", "dp", None, None), P("ctx", "dp", None, None)),
        check_vma=False,
    )
```

```python
import jax
import jax.numpy as jnp
from jax import lax
from jax.experimental import pallas as pl
from jax.experimental.pallas import tpu as pltpu
from jax.sharding import PartitionSpec as P

damping = 1.0

NX, NY, NZ = 4, 8, 8
ROWS = 160
HALF = ROWS // 2
W = 2048
HW = W // 2
BLK = 128
NB = HW // BLK
TOKENS = ROWS * 2 * NX * NY * NZ
MESH = pl.DeviceIdType.MESH

STREAMS = ((0, 1, 4), (0, -1, 3), (1, 1, 3), (1, -1, 4))
BASE = (0, 4, 7, 10)
NSLOT = 14
CHUNK = 256
CODE_TOP = 2.0 ** 15


def device(x, y, z, c):
    return (x * (NZ // 2) + z // 2, (z % 2) * (2 * NY) + y * 2 + c)


def kernel(act, grad, act_out, grad_out,
           xb, pk, q1, r1, r2, outbox, inbox, dg, gy, gz, gx, gc,
           loc_sem, raw_s, raw_r, s1_s, s1_r, s2_s, s2_r,
           dg_s, dg_r, out_s, out_r):
    dp = lax.axis_index("dp")
    ctx = lax.axis_index("ctx")
    x = dp // (NZ // 2)
    z = (dp % (NZ // 2)) * 2 + ctx // (2 * NY)
    y = (ctx // 2) % NY
    c = ctx % 2
    par = x % 2

    def at_x(d):
        return device((x + d) % NX, y, z, c)

    def at_y(d):
        return device(x, (y + d) % NY, z, c)

    def at_z(d):
        return device(x, y, (z + d) % NZ, c)

    partner = device(x, y, z, 1 - c)

    def remote(src, dst, ssem, rsem, dev):
        return pltpu.make_async_remote_copy(
            src_ref=src, dst_ref=dst, send_sem=ssem, recv_sem=rsem,
            device_id=dev, device_id_type=MESH)

    barrier = pltpu.get_barrier_semaphore()
    peers = [partner] + [at_x(d) for d in range(1, NX)]
    peers += [at_y(d) for d in range(1, NY)] + [at_z(d) for d in range(1, NZ)]
    for dev in peers:
        pl.semaphore_signal(barrier, inc=1, device_id=dev, device_id_type=MESH)

    own_rows = xb.at[pl.ds(0, ROWS)]

    @pl.when(par == 0)
    def _():
        pltpu.make_async_copy(act, own_rows, loc_sem).start()

    @pl.when(par == 1)
    def _():
        pltpu.make_async_copy(grad, own_rows, loc_sem).start()

    pl.semaphore_wait(barrier, len(peers))

    def raw_copies(own, other):
        copies = []
        for h in range(2):
            cols = pl.ds(h * HW, HW)
            copies.append(remote(
                other.at[pl.ds(0, HALF), cols],
                xb.at[pl.ds(2 * ROWS, HALF), cols],
                raw_s.at[2 * h], raw_r.at[2 * h], at_x(1)))
            copies.append(remote(
                other.at[pl.ds(HALF, HALF), cols],
                xb.at[pl.ds(2 * ROWS + HALF, HALF), cols],
                raw_s.at[2 * h + 1], raw_r.at[2 * h + 1], at_x(-1)))
        copies.append(remote(own, xb.at[pl.ds(ROWS, ROWS)],
                             raw_s.at[4], raw_r.at[4], partner))
        return copies

    @pl.when(par == 0)
    def _():
        for copy in raw_copies(act, grad):
            copy.start()

    @pl.when(par == 1)
    def _():
        for copy in raw_copies(grad, act):
            copy.start()

    raw = raw_copies(act, grad)
    pltpu.make_async_copy(act, own_rows, loc_sem).wait()
    raw[4].wait_recv()

    contract = (((0,), (0,)), ((), ()))

    def product(rows, left, right):
        return lax.dot_general(xb[rows, left], xb[rows, right], contract,
                               preferred_element_type=jnp.float32)

    upper = (lax.broadcasted_iota(jnp.int32, (256, 256), 0)
             < lax.broadcasted_iota(jnp.int32, (256, 256), 1))

    def store(a, b, value, add):
        for i in range(2):
            for j in range(2):
                part = value[BLK * i:BLK * (i + 1), BLK * j:BLK * (j + 1)]
                if add:
                    part = part + pk[2 * a + i, 2 * b + j]
                pk[2 * a + i, 2 * b + j] = part

    def tile_grid(row, add):
        rows = pl.ds(row, 2 * ROWS)

        @pl.when(c == 0)
        def _():
            for a in range(4):
                value = product(rows, pl.ds(256 * a, 256), pl.ds(HW, HW))
                for b in range(4):
                    store(a, b, value[:, 256 * b:256 * (b + 1)], add)

        @pl.when(c == 1)
        def _():
            for a in range(4):
                first = product(rows, pl.ds(256 * a, 256), pl.ds(256 * a, HW - 256 * a))
                second = product(rows, pl.ds(HW + 256 * a, 256), pl.ds(HW, 256 * (a + 1)))
                for b in range(4):
                    high = first[:, 256 * (b - a):256 * (b - a + 1)] if b >= a else None
                    low = second[:, 256 * b:256 * (b + 1)] if b <= a else None
                    if high is None:
                        store(a, b, low, add)
                    elif low is None:
                        store(a, b, high, add)
                    else:
                        store(a, b, jnp.where(upper, high, low), add)

    tile_grid(0, False)

    relay = []
    for h in range(2):
        for s in range(2):
            raw[2 * h + s].wait_recv()
            rows = pl.ds(2 * ROWS + HALF * s, HALF)
            to = pl.ds(3 * ROWS + HALF * s, HALF)
            cols = pl.ds(h * HW, HW)
            copy = remote(xb.at[rows, cols], xb.at[to, cols],
                          raw_s.at[5 + 2 * h + s], raw_r.at[5 + 2 * h + s], partner)
            copy.start()
            relay.append(copy)
    for copy in relay:
        copy.wait_recv()

    tile_grid(2 * ROWS, True)

    def chunk1(k, o, h):
        if k == 0:
            return pk.at[o, pl.ds(4 * h, 4), pl.ds(0, 64), :]
        return pk.at[pl.ds(4 * h, 4), o, pl.ds(64, 64), :]

    def encode(value, ref):
        n = value.shape[0]
        tiles = value.reshape(n // 8, 8, BLK)
        top = jnp.max(jnp.abs(tiles), axis=0)
        scale = (CODE_TOP / jnp.maximum(top, 1e-30)).astype(jnp.bfloat16)
        v = tiles * scale.astype(jnp.float32)[None]
        for _ in range(3):
            v = v * jnp.abs(v)
        ref[pl.ds(0, n), :] = v.reshape(n, BLK).astype(jnp.bfloat16)
        ref[pl.ds(n, 16), :] = jnp.concatenate([scale, scale], axis=0)

    def decode(ref, n):
        y = ref[pl.ds(0, n), :].astype(jnp.float32).reshape(n // 8, 8, BLK)
        inverse = 1.0 / ref[pl.ds(n, 16), :].astype(jnp.float32)[0:8]
        root = lax.rsqrt(lax.rsqrt(jnp.maximum(jnp.abs(y), 1.2e-38)))
        root = root * lax.rsqrt(root)
        return (jnp.where(y < 0, -root, root) * inverse[None]).reshape(n, BLK)

    def ring(chunk, sent, slots, ssem, rsem, axes, between):
        copies = {}
        for t in range(5):
            for i, (h, sign, hops) in enumerate(STREAMS):
                if t > hops:
                    continue
                for k in range(2):
                    pos, at = axes[k]
                    o = (pos + sign * (hops - t)) % NY
                    ref = chunk(k, o, h)
                    value = ref[...].reshape(CHUNK, BLK)
                    if t > 0:
                        copies[k, i, t - 1].wait_recv()
                        value = value + decode(slots.at[k * NSLOT + BASE[i] + t - 1], CHUNK)
                    if t == hops:
                        ref[...] = value.reshape(4, 64, BLK)
                    else:
                        slot = k * NSLOT + BASE[i] + t
                        encode(value, sent.at[slot])
                        copy = remote(sent.at[slot], slots.at[slot], ssem.at[slot],
                                      rsem.at[slot], at(sign))
                        copy.start()
                        copies[k, i, t] = copy
            between(t)
        return copies

    diag_copies = []

    def diag_send(srcs, dsts, devs, base):
        copies = []
        for n, (src, dst, dev) in enumerate(zip(srcs, dsts, devs)):
            copy = remote(src, dst, dg_s.at[base + n], dg_r.at[base + n], dev)
            copy.start()
            copies.append(copy)
        diag_copies.extend(copies)
        return copies

    pending = {}

    def between1(t):
        if t == 0:
            for i in range(NB):
                cols = pl.ds(pl.multiple_of(c * HW + BLK * i, BLK), BLK)
                part = xb[:, cols].astype(jnp.float32)
                dg[0, pl.ds(i, 1), :] = jnp.sum(part * part, axis=0, keepdims=True)
            pending["y"] = diag_send(
                [dg.at[0]] * 7, [gy.at[d - 1] for d in range(1, NY)],
                [at_y(d) for d in range(1, NY)], 0)
        elif t == 1:
            total = dg[0]
            for d in range(7):
                pending["y"][d].wait_recv()
                total = total + gy[d]
            dg[1] = total
            pending["z"] = diag_send(
                [dg.at[1]] * 7, [gz.at[d - 1] for d in range(1, NZ)],
                [at_z(d) for d in range(1, NZ)], 7)
        elif t == 2:
            total = dg[1]
            for d in range(7):
                pending["z"][d].wait_recv()
                total = total + gz[d]
            gx[x] = total
            pending["x"] = diag_send(
                [gx.at[x]] * 3, [gx.at[x]] * 3,
                [at_x(d) for d in range(1, NX)], 14)
        elif t == 3:
            for d in range(1, NX):
                src = (x - d) % NX
                remote(gx.at[src], gx.at[src], dg_s.at[13 + d], dg_r.at[13 + d],
                       at_x(d)).wait_recv()
            pending["c"] = diag_send([gx], [gc], [partner], 17)
        else:
            pending["c"][0].wait_recv()

    first = ring(chunk1, q1, r1, s1_s, s1_r, ((y, at_y), (z, at_z)), between1)
    second = []
    for d in (4, 3, 5, 2, 6, 1, 7):
        for k in range(2):
            if k == 0:
                src, dev = pk.at[y, (z + d) % NZ, pl.ds(0, 64), :], at_z(d)
            else:
                src, dev = pk.at[(y + d) % NY, z, pl.ds(64, 64), :], at_y(d)
            slot = 7 * k + d - 1
            copy = remote(src, r2.at[slot], s2_s.at[slot], s2_r.at[slot], dev)
            copy.start()
            second.append((k, slot, copy))
    sums = [pk[y, z, pl.ds(0, 64), :], pk[y, z, pl.ds(64, 64), :]]
    for k, slot, copy in sorted(second, key=lambda e: min(e[1] % 7, 6 - e[1] % 7)):
        copy.wait_recv()
        sums[k] = sums[k] + r2[slot]

    piece = jnp.concatenate(sums, axis=0)
    flipped = piece.T
    below = (lax.broadcasted_iota(jnp.int32, (BLK, BLK), 0)
             > lax.broadcasted_iota(jnp.int32, (BLK, BLK), 1))
    packed = jnp.logical_and(c == 1, y == z)
    swap = jnp.logical_and(below, packed)
    outbox[0] = jnp.where(swap, flipped, piece)
    outbox[1] = jnp.where(swap, piece, flipped)

    off_a = jnp.where(y > z, NB, 0)
    off_b = jnp.where(y >= z, NB, 0)
    blocks = (
        (y + jnp.where(c == 0, 0, off_a), z + jnp.where(c == 0, NB, off_a)),
        (z + jnp.where(c == 0, NB, off_b), y + jnp.where(c == 0, 0, off_b)),
    )
    me = (dp, ctx)
    sends = []
    for g in range(2):
        bi, bj = blocks[g]
        slot = par * 8 + (x // 2) * 4 + bj % 4
        for s in range(8):
            dev = device(2 * (bi % 2) + s // 4, 2 * (bj // 4) + (bi // 4) % 2,
                         2 * (s % 4) + bi // 8, (bi // 2) % 2)
            is_me = jnp.logical_and(dev[0] == me[0], dev[1] == me[1])
            src = outbox.at[g, pl.ds(16 * s, 16), :]
            dst = inbox.at[slot]
            copy = remote(src, dst, out_s.at[8 * g + s], out_r.at[slot], dev)

            @pl.when(is_me)
            def _():
                pltpu.make_async_copy(src, dst, out_r.at[slot]).start()

            @pl.when(jnp.logical_not(is_me))
            def _():
                copy.start()
            sends.append((copy, is_me))

    mine = [gx[n] for n in range(NX)]
    theirs = [gc[n] for n in range(NX)]
    diag = [(mine[f] + mine[f + 2], theirs[f] + theirs[f + 2]) for f in range(2)]
    row_block = (z % 2) * 8 + (y % 2) * 4 + c * 2 + x // 2
    strip = (x % 2) * 4 + z // 2
    own_half = (row_block // 8) == c
    pick = lax.broadcasted_iota(jnp.int32, (8, BLK), 0) == row_block % 8
    trace = []
    values = []
    for a, b in diag:
        trace.append(jnp.sum(a + b, keepdims=True))
        chosen = jnp.where(own_half, a, b)
        values.append(jnp.sum(jnp.where(pick, chosen, 0.0), axis=0, keepdims=True))
    ratio = jnp.sqrt(trace[0] / trace[1])
    shift = (ratio * damping, damping / ratio)
    scale = 1.0 / TOKENS
    on_diag = (lax.broadcasted_iota(jnp.int32, (16, BLK), 1)
               == lax.broadcasted_iota(jnp.int32, (16, BLK), 0) + 16 * strip)
    for f in range(2):
        out = (act_out, grad_out)[f]
        damped = values[f] * scale + shift[f]
        for j in range(4):
            for n in range(2):
                slot = 8 * f + 4 * n + j
                pltpu.make_async_copy(outbox.at[0, pl.ds(0, 16), :], inbox.at[slot],
                                      out_r.at[slot]).wait()
            here = jnp.logical_and(on_diag, (y // 2) * 4 + j == row_block)
            value = (inbox[8 * f + j] + inbox[8 * f + 4 + j]) * scale
            out[:, BLK * j:BLK * (j + 1)] = jnp.where(here, damped, value)

    for copy, is_me in sends:
        @pl.when(jnp.logical_not(is_me))
        def _():
            copy.wait_send()
    for copy in raw + relay + list(first.values()) + [copy for _, _, copy in second] + diag_copies:
        copy.wait_send()


def on_device(act_input, out_grad):
    f32 = jnp.float32
    piece = jax.ShapeDtypeStruct((16, 4 * BLK), f32)
    any_space = pl.BlockSpec(memory_space=pltpu.HBM)
    vmem = pl.BlockSpec(memory_space=pltpu.VMEM)
    dma = pltpu.SemaphoreType.DMA
    act_out, grad_out = pl.pallas_call(
        kernel,
        out_shape=(piece, piece),
        in_specs=[any_space, any_space],
        out_specs=(vmem, vmem),
        scratch_shapes=[
            pltpu.VMEM((4 * ROWS, W), jnp.bfloat16),
            pltpu.VMEM((NB, NB, BLK, BLK), f32),
            pltpu.VMEM((2 * NSLOT, CHUNK + 16, BLK), jnp.bfloat16),
            pltpu.VMEM((2 * NSLOT, CHUNK + 16, BLK), jnp.bfloat16),
            pltpu.VMEM((14, 64, BLK), f32),
            pltpu.VMEM((2, BLK, BLK), f32),
            pltpu.VMEM((16, 16, BLK), f32),
            pltpu.VMEM((2, 8, BLK), f32),
            pltpu.VMEM((7, 8, BLK), f32),
            pltpu.VMEM((7, 8, BLK), f32),
            pltpu.VMEM((NX, 8, BLK), f32),
            pltpu.VMEM((NX, 8, BLK), f32),
            dma,
            dma((9,)), dma((9,)),
            dma((2 * NSLOT,)), dma((2 * NSLOT,)),
            dma((2 * NSLOT,)), dma((2 * NSLOT,)),
            dma((18,)), dma((18,)),
            dma((16,)), dma((16,)),
        ],
        compiler_params=pltpu.CompilerParams(
            collective_id=0, has_side_effects=True,
            vmem_limit_bytes=62 * 1024 * 1024),
        name="kfac",
    )(act_input, out_grad)
    return act_out[None, None], grad_out[None, None]


def solution(mesh):
    placed = (P(("dp", "ctx"), None), P(("dp", "ctx"), None))
    return jax.shard_map(
        on_device,
        mesh=mesh,
        in_specs=placed,
        out_specs=(P("ctx", "dp", None, None), P("ctx", "dp", None, None)),
        check_vma=False,
    )
```

```python
import jax
import jax.numpy as jnp
from jax import lax
from jax.experimental import pallas as pl
from jax.experimental.pallas import tpu as pltpu
from jax.sharding import PartitionSpec as P

damping = 1.0

NX, NY, NZ = 4, 8, 8
ROWS = 160
HALF = ROWS // 2
W = 2048
HW = W // 2
BLK = 128
NB = HW // BLK
TOKENS = ROWS * 2 * NX * NY * NZ
MESH = pl.DeviceIdType.MESH

STREAMS = ((0, 1, 4), (1, -1, 4), (2, 1, 4), (3, -1, 4),
           (1, 1, 3), (0, -1, 3), (3, 1, 3), (2, -1, 3))
BASE = (0, 4, 8, 12, 16, 19, 22, 25)
NSLOT = 28
RAW = 2
CHUNK = 128
CODE_TOP = 2.0 ** 15


def device(x, y, z, c):
    return (x * (NZ // 2) + z // 2, (z % 2) * (2 * NY) + y * 2 + c)


def kernel(act, grad, act_out, grad_out,
           xb, pk, q1, r1, q2, r2, outbox, inbox, dg, gy, gz, gx, gc,
           loc_sem, raw_s, raw_r, s1_s, s1_r, s2_s, s2_r,
           dg_s, dg_r, out_s, out_r):
    dp = lax.axis_index("dp")
    ctx = lax.axis_index("ctx")
    x = dp // (NZ // 2)
    z = (dp % (NZ // 2)) * 2 + ctx // (2 * NY)
    y = (ctx // 2) % NY
    c = ctx % 2
    par = x % 2

    def at_x(d):
        return device((x + d) % NX, y, z, c)

    def at_y(d):
        return device(x, (y + d) % NY, z, c)

    def at_z(d):
        return device(x, y, (z + d) % NZ, c)

    partner = device(x, y, z, 1 - c)

    def remote(src, dst, ssem, rsem, dev):
        return pltpu.make_async_remote_copy(
            src_ref=src, dst_ref=dst, send_sem=ssem, recv_sem=rsem,
            device_id=dev, device_id_type=MESH)

    barrier = pltpu.get_barrier_semaphore()
    peers = [partner] + [at_x(d) for d in range(1, NX)]
    peers += [at_y(d) for d in range(1, NY)] + [at_z(d) for d in range(1, NZ)]
    for dev in peers:
        pl.semaphore_signal(barrier, inc=1, device_id=dev, device_id_type=MESH)

    own_rows = xb.at[pl.ds(0, ROWS)]

    @pl.when(par == 0)
    def _():
        pltpu.make_async_copy(act, own_rows, loc_sem).start()

    @pl.when(par == 1)
    def _():
        pltpu.make_async_copy(grad, own_rows, loc_sem).start()

    pl.semaphore_wait(barrier, len(peers))

    def raw_copies(own, other):
        copies = []
        for h in range(RAW):
            cols = pl.ds(h * (W // RAW), W // RAW)
            copies.append(remote(
                other.at[pl.ds(0, HALF), cols],
                xb.at[pl.ds(2 * ROWS, HALF), cols],
                raw_s.at[2 * h], raw_r.at[2 * h], at_x(1)))
            copies.append(remote(
                other.at[pl.ds(HALF, HALF), cols],
                xb.at[pl.ds(2 * ROWS + HALF, HALF), cols],
                raw_s.at[2 * h + 1], raw_r.at[2 * h + 1], at_x(-1)))
        copies.append(remote(own, xb.at[pl.ds(ROWS, ROWS)],
                             raw_s.at[2 * RAW], raw_r.at[2 * RAW], partner))
        return copies

    @pl.when(par == 0)
    def _():
        for copy in raw_copies(act, grad):
            copy.start()

    @pl.when(par == 1)
    def _():
        for copy in raw_copies(grad, act):
            copy.start()

    raw = raw_copies(act, grad)
    pltpu.make_async_copy(act, own_rows, loc_sem).wait()
    raw[2 * RAW].wait_recv()

    contract = (((0,), (0,)), ((), ()))

    def product(rows, left, right):
        return lax.dot_general(xb[rows, left], xb[rows, right], contract,
                               preferred_element_type=jnp.float32)

    upper = (lax.broadcasted_iota(jnp.int32, (256, 256), 0)
             < lax.broadcasted_iota(jnp.int32, (256, 256), 1))

    def store(a, b, value, add):
        for i in range(2):
            for j in range(2):
                part = value[BLK * i:BLK * (i + 1), BLK * j:BLK * (j + 1)]
                if add:
                    part = part + pk[2 * a + i, 2 * b + j]
                pk[2 * a + i, 2 * b + j] = part

    def tile_grid(row, add):
        rows = pl.ds(row, 2 * ROWS)

        @pl.when(c == 0)
        def _():
            for a in range(4):
                value = product(rows, pl.ds(256 * a, 256), pl.ds(HW, HW))
                for b in range(4):
                    store(a, b, value[:, 256 * b:256 * (b + 1)], add)

        @pl.when(c == 1)
        def _():
            for a in range(4):
                first = product(rows, pl.ds(256 * a, 256), pl.ds(256 * a, HW - 256 * a))
                second = product(rows, pl.ds(HW + 256 * a, 256), pl.ds(HW, 256 * (a + 1)))
                for b in range(4):
                    high = first[:, 256 * (b - a):256 * (b - a + 1)] if b >= a else None
                    low = second[:, 256 * b:256 * (b + 1)] if b <= a else None
                    if high is None:
                        store(a, b, low, add)
                    elif low is None:
                        store(a, b, high, add)
                    else:
                        store(a, b, jnp.where(upper, high, low), add)

    tile_grid(0, False)

    relay = []
    for h in range(RAW):
        for s in range(2):
            raw[2 * h + s].wait_recv()
            rows = pl.ds(2 * ROWS + HALF * s, HALF)
            to = pl.ds(3 * ROWS + HALF * s, HALF)
            cols = pl.ds(h * (W // RAW), W // RAW)
            slot = 2 * RAW + 1 + 2 * h + s
            copy = remote(xb.at[rows, cols], xb.at[to, cols],
                          raw_s.at[slot], raw_r.at[slot], partner)
            copy.start()
            relay.append(copy)
    for copy in relay:
        copy.wait_recv()

    tile_grid(2 * ROWS, True)

    def chunk1(k, o, h):
        if k == 0:
            return pk.at[o, pl.ds(2 * h, 2), pl.ds(0, 64), :]
        return pk.at[pl.ds(2 * h, 2), o, pl.ds(64, 64), :]

    def encode(value, ref):
        n = value.shape[0]
        tiles = value.reshape(n // 8, 8, BLK)
        top = jnp.max(jnp.abs(tiles), axis=0)
        scale = (CODE_TOP / jnp.maximum(top, 1e-30)).astype(jnp.bfloat16)
        v = tiles * scale.astype(jnp.float32)[None]
        for _ in range(3):
            v = v * jnp.abs(v)
        ref[pl.ds(0, n), :] = v.reshape(n, BLK).astype(jnp.bfloat16)
        ref[pl.ds(n, 16), :] = jnp.concatenate([scale, scale], axis=0)

    def decode(ref, n):
        y = ref[pl.ds(0, n), :].astype(jnp.float32).reshape(n // 8, 8, BLK)
        inverse = 1.0 / ref[pl.ds(n, 16), :].astype(jnp.float32)[0:8]
        root = lax.rsqrt(lax.rsqrt(jnp.maximum(jnp.abs(y), 1.2e-38)))
        root = root * lax.rsqrt(root)
        return (jnp.where(y < 0, -root, root) * inverse[None]).reshape(n, BLK)

    def ring(chunk, sent, slots, ssem, rsem, axes, between):
        copies = {}
        for t in range(5):
            for i, (h, sign, hops) in enumerate(STREAMS):
                if t > hops:
                    continue
                for k in range(2):
                    pos, at = axes[k]
                    o = (pos + sign * (hops - t)) % NY
                    ref = chunk(k, o, h)
                    value = ref[...].reshape(CHUNK, BLK)
                    if t > 0:
                        copies[k, i, t - 1].wait_recv()
                        value = value + decode(slots.at[k * NSLOT + BASE[i] + t - 1], CHUNK)
                    if t == hops:
                        ref[...] = value.reshape(2, 64, BLK)
                    else:
                        slot = k * NSLOT + BASE[i] + t
                        encode(value, sent.at[slot])
                        copy = remote(sent.at[slot], slots.at[slot], ssem.at[slot],
                                      rsem.at[slot], at(sign))
                        copy.start()
                        copies[k, i, t] = copy
            between(t)
        return copies

    diag_copies = []

    def diag_send(srcs, dsts, devs, base):
        copies = []
        for n, (src, dst, dev) in enumerate(zip(srcs, dsts, devs)):
            copy = remote(src, dst, dg_s.at[base + n], dg_r.at[base + n], dev)
            copy.start()
            copies.append(copy)
        diag_copies.extend(copies)
        return copies

    pending = {}

    def between1(t):
        if t == 0:
            for i in range(NB):
                cols = pl.ds(pl.multiple_of(c * HW + BLK * i, BLK), BLK)
                part = xb[:, cols].astype(jnp.float32)
                dg[0, pl.ds(i, 1), :] = jnp.sum(part * part, axis=0, keepdims=True)
            pending["y"] = diag_send(
                [dg.at[0]] * 7, [gy.at[d - 1] for d in range(1, NY)],
                [at_y(d) for d in range(1, NY)], 0)
        elif t == 2:
            total = dg[0]
            for d in range(7):
                pending["y"][d].wait_recv()
                total = total + gy[d]
            dg[1] = total
            pending["z"] = diag_send(
                [dg.at[1]] * 7, [gz.at[d - 1] for d in range(1, NZ)],
                [at_z(d) for d in range(1, NZ)], 7)

    def diag_finish():
        total = dg[1]
        for d in range(7):
            pending["z"][d].wait_recv()
            total = total + gz[d]
        gx[x] = total
        diag_send([gx.at[x]] * 3, [gx.at[x]] * 3, [at_x(d) for d in range(1, NX)], 14)

    def diag_share():
        for d in range(1, NX):
            src = (x - d) % NX
            remote(gx.at[src], gx.at[src], dg_s.at[13 + d], dg_r.at[13 + d],
                   at_x(d)).wait_recv()
        return diag_send([gx], [gc], [partner], 17)[0]

    first = ring(chunk1, q1, r1, s1_s, s1_r, ((y, at_y), (z, at_z)), between1)
    second = []
    for d in (4, 3, 5, 2, 6, 1, 7):
        for k in range(2):
            if k == 0:
                value, dev = pk[y, (z + d) % NZ, pl.ds(0, 64), :], at_z(d)
            else:
                value, dev = pk[(y + d) % NY, z, pl.ds(64, 64), :], at_y(d)
            slot = 7 * k + d - 1
            encode(value, q2.at[slot])
            copy = remote(q2.at[slot], r2.at[slot], s2_s.at[slot], s2_r.at[slot], dev)
            copy.start()
            second.append((k, slot, copy))
    diag_finish()
    shared = diag_share()
    sums = [pk[y, z, pl.ds(0, 64), :], pk[y, z, pl.ds(64, 64), :]]
    for k, slot, copy in sorted(second, key=lambda e: min(e[1] % 7, 6 - e[1] % 7)):
        copy.wait_recv()
        sums[k] = sums[k] + decode(r2.at[slot], 64)
    shared.wait_recv()

    piece = jnp.concatenate(sums, axis=0)
    flipped = piece.T
    below = (lax.broadcasted_iota(jnp.int32, (BLK, BLK), 0)
             > lax.broadcasted_iota(jnp.int32, (BLK, BLK), 1))
    packed = jnp.logical_and(c == 1, y == z)
    swap = jnp.logical_and(below, packed)
    outbox[0] = jnp.where(swap, flipped, piece)
    outbox[1] = jnp.where(swap, piece, flipped)

    off_a = jnp.where(y > z, NB, 0)
    off_b = jnp.where(y >= z, NB, 0)
    blocks = (
        (y + jnp.where(c == 0, 0, off_a), z + jnp.where(c == 0, NB, off_a)),
        (z + jnp.where(c == 0, NB, off_b), y + jnp.where(c == 0, 0, off_b)),
    )
    me = (dp, ctx)
    sends = []
    for g in range(2):
        bi, bj = blocks[g]
        slot = par * 8 + (x // 2) * 4 + bj % 4
        for s in range(8):
            dev = device(2 * (bi % 2) + s // 4, 2 * (bj // 4) + (bi // 4) % 2,
                         2 * (s % 4) + bi // 8, (bi // 2) % 2)
            is_me = jnp.logical_and(dev[0] == me[0], dev[1] == me[1])
            src = outbox.at[g, pl.ds(16 * s, 16), :]
            dst = inbox.at[slot]
            copy = remote(src, dst, out_s.at[8 * g + s], out_r.at[slot], dev)

            @pl.when(is_me)
            def _():
                pltpu.make_async_copy(src, dst, out_r.at[slot]).start()

            @pl.when(jnp.logical_not(is_me))
            def _():
                copy.start()
            sends.append((copy, is_me))

    mine = [gx[n] for n in range(NX)]
    theirs = [gc[n] for n in range(NX)]
    diag = [(mine[f] + mine[f + 2], theirs[f] + theirs[f + 2]) for f in range(2)]
    row_block = (z % 2) * 8 + (y % 2) * 4 + c * 2 + x // 2
    strip = (x % 2) * 4 + z // 2
    own_half = (row_block // 8) == c
    pick = lax.broadcasted_iota(jnp.int32, (8, BLK), 0) == row_block % 8
    trace = []
    values = []
    for a, b in diag:
        trace.append(jnp.sum(a + b, keepdims=True))
        chosen = jnp.where(own_half, a, b)
        values.append(jnp.sum(jnp.where(pick, chosen, 0.0), axis=0, keepdims=True))
    ratio = jnp.sqrt(trace[0] / trace[1])
    shift = (ratio * damping, damping / ratio)
    scale = 1.0 / TOKENS
    on_diag = (lax.broadcasted_iota(jnp.int32, (16, BLK), 1)
               == lax.broadcasted_iota(jnp.int32, (16, BLK), 0) + 16 * strip)
    for f in range(2):
        out = (act_out, grad_out)[f]
        damped = values[f] * scale + shift[f]
        for j in range(4):
            for n in range(2):
                slot = 8 * f + 4 * n + j
                pltpu.make_async_copy(outbox.at[0, pl.ds(0, 16), :], inbox.at[slot],
                                      out_r.at[slot]).wait()
            here = jnp.logical_and(on_diag, (y // 2) * 4 + j == row_block)
            value = (inbox[8 * f + j] + inbox[8 * f + 4 + j]) * scale
            out[:, BLK * j:BLK * (j + 1)] = jnp.where(here, damped, value)

    for copy, is_me in sends:
        @pl.when(jnp.logical_not(is_me))
        def _():
            copy.wait_send()
    for copy in raw + relay + list(first.values()) + [copy for _, _, copy in second] + diag_copies:
        copy.wait_send()


def on_device(act_input, out_grad):
    f32 = jnp.float32
    piece = jax.ShapeDtypeStruct((16, 4 * BLK), f32)
    any_space = pl.BlockSpec(memory_space=pltpu.HBM)
    vmem = pl.BlockSpec(memory_space=pltpu.VMEM)
    dma = pltpu.SemaphoreType.DMA
    act_out, grad_out = pl.pallas_call(
        kernel,
        out_shape=(piece, piece),
        in_specs=[any_space, any_space],
        out_specs=(vmem, vmem),
        scratch_shapes=[
            pltpu.VMEM((4 * ROWS, W), jnp.bfloat16),
            pltpu.VMEM((NB, NB, BLK, BLK), f32),
            pltpu.VMEM((2 * NSLOT, CHUNK + 16, BLK), jnp.bfloat16),
            pltpu.VMEM((2 * NSLOT, CHUNK + 16, BLK), jnp.bfloat16),
            pltpu.VMEM((14, 80, BLK), jnp.bfloat16),
            pltpu.VMEM((14, 80, BLK), jnp.bfloat16),
            pltpu.VMEM((2, BLK, BLK), f32),
            pltpu.VMEM((16, 16, BLK), f32),
            pltpu.VMEM((2, 8, BLK), f32),
            pltpu.VMEM((7, 8, BLK), f32),
            pltpu.VMEM((7, 8, BLK), f32),
            pltpu.VMEM((NX, 8, BLK), f32),
            pltpu.VMEM((NX, 8, BLK), f32),
            dma,
            dma((4 * RAW + 1,)), dma((4 * RAW + 1,)),
            dma((2 * NSLOT,)), dma((2 * NSLOT,)),
            dma((2 * NSLOT,)), dma((2 * NSLOT,)),
            dma((18,)), dma((18,)),
            dma((16,)), dma((16,)),
        ],
        compiler_params=pltpu.CompilerParams(
            collective_id=0, has_side_effects=True,
            vmem_limit_bytes=62 * 1024 * 1024),
        name="kfac",
    )(act_input, out_grad)
    return act_out[None, None], grad_out[None, None]


def solution(mesh):
    placed = (P(("dp", "ctx"), None), P(("dp", "ctx"), None))
    return jax.shard_map(
        on_device,
        mesh=mesh,
        in_specs=placed,
        out_specs=(P("ctx", "dp", None, None), P("ctx", "dp", None, None)),
        check_vma=False,
    )
```

```python
import jax
import jax.numpy as jnp
from jax import lax
from jax.experimental import pallas as pl
from jax.experimental.pallas import tpu as pltpu
from jax.sharding import PartitionSpec as P

damping = 1.0

NX, NY, NZ = 4, 8, 8
ROWS = 160
HALF = ROWS // 2
W = 2048
HW = W // 2
BLK = 128
NB = HW // BLK
TOKENS = ROWS * 2 * NX * NY * NZ
MESH = pl.DeviceIdType.MESH

STREAMS = ((0, 1, 4), (1, -1, 4), (2, 1, 4), (3, -1, 4),
           (1, 1, 3), (0, -1, 3), (3, 1, 3), (2, -1, 3))
BASE = (0, 4, 8, 12, 16, 19, 22, 25)
NSLOT = 28
RAW = 2
CHUNK = 128
CODE_TOP = 2.0 ** 15


def device(x, y, z, c):
    return (x * (NZ // 2) + z // 2, (z % 2) * (2 * NY) + y * 2 + c)


def kernel(act, grad, act_out, grad_out,
           xb, ob, pk, q1, r1, q2, r2, outbox, inbox, dl, dg, gd, gy, gz, gx, gc,
           loc_sem, raw_s, raw_r, s1_s, s1_r, s2_s, s2_r,
           dg_s, dg_r, out_s, out_r):
    dp = lax.axis_index("dp")
    ctx = lax.axis_index("ctx")
    x = dp // (NZ // 2)
    z = (dp % (NZ // 2)) * 2 + ctx // (2 * NY)
    y = (ctx // 2) % NY
    c = ctx % 2
    par = x % 2

    def at_x(d):
        return device((x + d) % NX, y, z, c)

    def at_y(d):
        return device(x, (y + d) % NY, z, c)

    def at_z(d):
        return device(x, y, (z + d) % NZ, c)

    partner = device(x, y, z, 1 - c)

    def remote(src, dst, ssem, rsem, dev):
        return pltpu.make_async_remote_copy(
            src_ref=src, dst_ref=dst, send_sem=ssem, recv_sem=rsem,
            device_id=dev, device_id_type=MESH)

    barrier = pltpu.get_barrier_semaphore()
    peers = [partner] + [at_x(d) for d in range(1, NX)]
    peers += [at_y(d) for d in range(1, NY)] + [at_z(d) for d in range(1, NZ)]
    for dev in peers:
        pl.semaphore_signal(barrier, inc=1, device_id=dev, device_id_type=MESH)

    own_rows = xb.at[pl.ds(0, ROWS)]

    @pl.when(par == 0)
    def _():
        pltpu.make_async_copy(act, own_rows, loc_sem.at[0]).start()
        pltpu.make_async_copy(grad, ob, loc_sem.at[1]).start()

    @pl.when(par == 1)
    def _():
        pltpu.make_async_copy(grad, own_rows, loc_sem.at[0]).start()
        pltpu.make_async_copy(act, ob, loc_sem.at[1]).start()

    pl.semaphore_wait(barrier, len(peers))

    def raw_copies(own, other):
        copies = []
        for h in range(RAW):
            cols = pl.ds(h * (W // RAW), W // RAW)
            copies.append(remote(
                other.at[pl.ds(0, HALF), cols],
                xb.at[pl.ds(2 * ROWS, HALF), cols],
                raw_s.at[2 * h], raw_r.at[2 * h], at_x(1)))
            copies.append(remote(
                other.at[pl.ds(HALF, HALF), cols],
                xb.at[pl.ds(2 * ROWS + HALF, HALF), cols],
                raw_s.at[2 * h + 1], raw_r.at[2 * h + 1], at_x(-1)))
        copies.append(remote(own, xb.at[pl.ds(ROWS, ROWS)],
                             raw_s.at[2 * RAW], raw_r.at[2 * RAW], partner))
        return copies

    @pl.when(par == 0)
    def _():
        for copy in raw_copies(act, grad):
            copy.start()

    @pl.when(par == 1)
    def _():
        for copy in raw_copies(grad, act):
            copy.start()

    raw = raw_copies(act, grad)
    pltpu.make_async_copy(act, own_rows, loc_sem.at[0]).wait()
    pltpu.make_async_copy(act, ob, loc_sem.at[1]).wait()

    diag_copies = []

    def diag_send(srcs, dsts, devs, base):
        copies = []
        for n, (src, dst, dev) in enumerate(zip(srcs, dsts, devs)):
            copy = remote(src, dst, dg_s.at[base + n], dg_r.at[base + n], dev)
            copy.start()
            copies.append(copy)
        diag_copies.extend(copies)
        return copies

    def diag_sum(first, copies, slots, to):
        total = dg[first]
        for n, copy in enumerate(copies):
            copy.wait_recv()
            total = total + slots[n]
        dg[to] = total

    for tokens, f in ((own_rows, par), (ob, 1 - par)):
        for i in range(2 * NB):
            part = tokens[:, BLK * i:BLK * (i + 1)].astype(jnp.float32)
            dl[i // NB, f, pl.ds(i % NB, 1), :] = jnp.sum(part * part, axis=0, keepdims=True)
    pending = {"d": diag_send([dl.at[1 - c]], [gd.at[0]], [partner], 0)}
    raw[2 * RAW].wait_recv()

    contract = (((0,), (0,)), ((), ()))

    def product(rows, left, right):
        return lax.dot_general(xb[rows, left], xb[rows, right], contract,
                               preferred_element_type=jnp.float32)

    upper = (lax.broadcasted_iota(jnp.int32, (256, 256), 0)
             < lax.broadcasted_iota(jnp.int32, (256, 256), 1))

    def store(a, b, value, add):
        for i in range(2):
            for j in range(2):
                part = value[BLK * i:BLK * (i + 1), BLK * j:BLK * (j + 1)]
                if add:
                    part = part + pk[2 * a + i, 2 * b + j]
                pk[2 * a + i, 2 * b + j] = part

    def tile_grid(row, add):
        rows = pl.ds(row, 2 * ROWS)

        @pl.when(c == 0)
        def _():
            for a in range(4):
                value = product(rows, pl.ds(256 * a, 256), pl.ds(HW, HW))
                for b in range(4):
                    store(a, b, value[:, 256 * b:256 * (b + 1)], add)

        @pl.when(c == 1)
        def _():
            for a in range(4):
                first = product(rows, pl.ds(256 * a, 256), pl.ds(256 * a, HW - 256 * a))
                second = product(rows, pl.ds(HW + 256 * a, 256), pl.ds(HW, 256 * (a + 1)))
                for b in range(4):
                    high = first[:, 256 * (b - a):256 * (b - a + 1)] if b >= a else None
                    low = second[:, 256 * b:256 * (b + 1)] if b <= a else None
                    if high is None:
                        store(a, b, low, add)
                    elif low is None:
                        store(a, b, high, add)
                    else:
                        store(a, b, jnp.where(upper, high, low), add)

    tile_grid(0, False)

    dg[0] = dl[c]
    diag_sum(0, pending["d"], gd, 0)
    pending["y"] = diag_send([dg.at[0]] * 7, [gy.at[d - 1] for d in range(1, NY)],
                             [at_y(d) for d in range(1, NY)], 1)

    relay = []
    for h in range(RAW):
        for s in range(2):
            raw[2 * h + s].wait_recv()
            rows = pl.ds(2 * ROWS + HALF * s, HALF)
            to = pl.ds(3 * ROWS + HALF * s, HALF)
            cols = pl.ds(h * (W // RAW), W // RAW)
            slot = 2 * RAW + 1 + 2 * h + s
            copy = remote(xb.at[rows, cols], xb.at[to, cols],
                          raw_s.at[slot], raw_r.at[slot], partner)
            copy.start()
            relay.append(copy)
    diag_sum(0, pending["y"], gy, 1)
    pending["z"] = diag_send([dg.at[1]] * 7, [gz.at[d - 1] for d in range(1, NZ)],
                             [at_z(d) for d in range(1, NZ)], 8)
    for copy in relay:
        copy.wait_recv()

    tile_grid(2 * ROWS, True)

    def chunk1(k, o, h):
        if k == 0:
            return pk.at[o, pl.ds(2 * h, 2), pl.ds(0, 64), :]
        return pk.at[pl.ds(2 * h, 2), o, pl.ds(64, 64), :]

    def power(v):
        for _ in range(3):
            v = v * jnp.abs(v)
        return v

    def root(y):
        r = lax.rsqrt(lax.rsqrt(jnp.maximum(jnp.abs(y), 1.2e-38)))
        r = r * lax.rsqrt(r)
        return jnp.where(y < 0, -r, r)

    def encode(value, ref):
        n = value.shape[0]
        tiles = value.reshape(n // 8, 8, BLK)
        top = jnp.max(jnp.abs(tiles), axis=0)
        scale = (CODE_TOP / jnp.maximum(top, 1e-30)).astype(jnp.bfloat16)
        y = power(tiles * scale.astype(jnp.float32)[None])
        ref[pl.ds(0, n), :] = y.reshape(n, BLK).astype(jnp.bfloat16)
        ref[pl.ds(n, 16), :] = jnp.concatenate([scale, scale], axis=0)

    def decode(ref, n):
        y = ref[pl.ds(0, n), :].astype(jnp.float32).reshape(n // 8, 8, BLK)
        inverse = 1.0 / ref[pl.ds(n, 16), :].astype(jnp.float32)[0:8]
        return (root(y) * inverse[None]).reshape(n, BLK)

    def ring(chunk, sent, slots, ssem, rsem, axes, between):
        copies = {}
        for t in range(5):
            for i, (h, sign, hops) in enumerate(STREAMS):
                if t > hops:
                    continue
                for k in range(2):
                    pos, at = axes[k]
                    o = (pos + sign * (hops - t)) % NY
                    ref = chunk(k, o, h)
                    value = ref[...].reshape(CHUNK, BLK)
                    if t > 0:
                        copies[k, i, t - 1].wait_recv()
                        value = value + decode(slots.at[k * NSLOT + BASE[i] + t - 1], CHUNK)
                    if t == hops:
                        ref[...] = value.reshape(2, 64, BLK)
                    else:
                        slot = k * NSLOT + BASE[i] + t
                        encode(value, sent.at[slot])
                        copy = remote(sent.at[slot], slots.at[slot], ssem.at[slot],
                                      rsem.at[slot], at(sign))
                        copy.start()
                        copies[k, i, t] = copy
            between(t)
        return copies

    def between1(t):
        if t == 1:
            diag_sum(1, pending["z"], gz, 2)
            pending["x"] = diag_send([dg.at[2]] * 3, [gx.at[d - 1] for d in range(1, NX)],
                                     [at_x(d) for d in range(1, NX)], 15)
        elif t == 2:
            diag_sum(2, pending["x"], gx, 3)
            pending["c"] = diag_send([dg.at[3]], [gc], [partner], 18)
        elif t == 3:
            pending["c"][0].wait_recv()

    first = ring(chunk1, q1, r1, s1_s, s1_r, ((y, at_y), (z, at_z)), between1)
    row_block = (z % 2) * 8 + (y % 2) * 4 + c * 2 + x // 2
    strip = (x % 2) * 4 + z // 2
    own_half = (row_block // 8) == c
    pick = lax.broadcasted_iota(jnp.int32, (8, BLK), 0) == row_block % 8
    trace = []
    values = []
    for f in range(2):
        a, b = dg[3, f], gc[f]
        trace.append(jnp.sum(a + b, keepdims=True))
        chosen = jnp.where(own_half, a, b)
        values.append(jnp.sum(jnp.where(pick, chosen, 0.0), axis=0, keepdims=True))
    bound = [jnp.maximum(t, 1e-30) for t in trace]
    my_bound = jnp.where(par == 0, bound[0], bound[1])
    to_code = CODE_TOP / my_bound
    from_code = my_bound / CODE_TOP

    second = []
    for d in (4, 3, 5, 2, 6, 1, 7):
        for k in range(2):
            if k == 0:
                value, dev = pk[y, (z + d) % NZ, pl.ds(0, 64), :], at_z(d)
            else:
                value, dev = pk[(y + d) % NY, z, pl.ds(64, 64), :], at_y(d)
            slot = 7 * k + d - 1
            q2[slot] = power(value * to_code).astype(jnp.bfloat16)
            copy = remote(q2.at[slot], r2.at[slot], s2_s.at[slot], s2_r.at[slot], dev)
            copy.start()
            second.append((k, slot, copy))
    sums = [pk[y, z, pl.ds(0, 64), :], pk[y, z, pl.ds(64, 64), :]]
    for k, slot, copy in sorted(second, key=lambda e: min(e[1] % 7, 6 - e[1] % 7)):
        copy.wait_recv()
        sums[k] = sums[k] + root(r2[slot].astype(jnp.float32)) * from_code

    piece = power(jnp.concatenate(sums, axis=0) * to_code)
    flipped = piece.T
    below = (lax.broadcasted_iota(jnp.int32, (BLK, BLK), 0)
             > lax.broadcasted_iota(jnp.int32, (BLK, BLK), 1))
    packed = jnp.logical_and(c == 1, y == z)
    swap = jnp.logical_and(below, packed)
    outbox[0] = jnp.where(swap, flipped, piece).astype(jnp.bfloat16)
    outbox[1] = jnp.where(swap, piece, flipped).astype(jnp.bfloat16)

    off_a = jnp.where(y > z, NB, 0)
    off_b = jnp.where(y >= z, NB, 0)
    blocks = (
        (y + jnp.where(c == 0, 0, off_a), z + jnp.where(c == 0, NB, off_a)),
        (z + jnp.where(c == 0, NB, off_b), y + jnp.where(c == 0, 0, off_b)),
    )
    me = (dp, ctx)
    sends = []
    for g in range(2):
        bi, bj = blocks[g]
        slot = par * 8 + (x // 2) * 4 + bj % 4
        for s in range(8):
            dev = device(2 * (bi % 2) + s // 4, 2 * (bj // 4) + (bi // 4) % 2,
                         2 * (s % 4) + bi // 8, (bi // 2) % 2)
            is_me = jnp.logical_and(dev[0] == me[0], dev[1] == me[1])
            src = outbox.at[g, pl.ds(16 * s, 16), :]
            dst = inbox.at[slot]
            copy = remote(src, dst, out_s.at[8 * g + s], out_r.at[slot], dev)

            @pl.when(is_me)
            def _():
                pltpu.make_async_copy(src, dst, out_r.at[slot]).start()

            @pl.when(jnp.logical_not(is_me))
            def _():
                copy.start()
            sends.append((copy, is_me))

    ratio = jnp.sqrt(trace[0] / trace[1])
    shift = (ratio * damping, damping / ratio)
    scale = 1.0 / TOKENS
    on_diag = (lax.broadcasted_iota(jnp.int32, (16, BLK), 1)
               == lax.broadcasted_iota(jnp.int32, (16, BLK), 0) + 16 * strip)
    for f in range(2):
        out = (act_out, grad_out)[f]
        damped = values[f] * scale + shift[f]
        for j in range(4):
            for n in range(2):
                slot = 8 * f + 4 * n + j
                pltpu.make_async_copy(outbox.at[0, pl.ds(0, 16), :], inbox.at[slot],
                                      out_r.at[slot]).wait()
            here = jnp.logical_and(on_diag, (y // 2) * 4 + j == row_block)
            value = (root(inbox[8 * f + j].astype(jnp.float32))
                     + root(inbox[8 * f + 4 + j].astype(jnp.float32)))
            value = value * (bound[f] * (scale / CODE_TOP))
            out[:, BLK * j:BLK * (j + 1)] = jnp.where(here, damped, value)

    for copy, is_me in sends:
        @pl.when(jnp.logical_not(is_me))
        def _():
            copy.wait_send()
    for copy in raw + relay + list(first.values()) + [copy for _, _, copy in second] + diag_copies:
        copy.wait_send()


def on_device(act_input, out_grad):
    f32 = jnp.float32
    piece = jax.ShapeDtypeStruct((16, 4 * BLK), f32)
    any_space = pl.BlockSpec(memory_space=pltpu.HBM)
    vmem = pl.BlockSpec(memory_space=pltpu.VMEM)
    dma = pltpu.SemaphoreType.DMA
    act_out, grad_out = pl.pallas_call(
        kernel,
        out_shape=(piece, piece),
        in_specs=[any_space, any_space],
        out_specs=(vmem, vmem),
        scratch_shapes=[
            pltpu.VMEM((4 * ROWS, W), jnp.bfloat16),
            pltpu.VMEM((ROWS, W), jnp.bfloat16),
            pltpu.VMEM((NB, NB, BLK, BLK), f32),
            pltpu.VMEM((2 * NSLOT, CHUNK + 16, BLK), jnp.bfloat16),
            pltpu.VMEM((2 * NSLOT, CHUNK + 16, BLK), jnp.bfloat16),
            pltpu.VMEM((14, 64, BLK), jnp.bfloat16),
            pltpu.VMEM((14, 64, BLK), jnp.bfloat16),
            pltpu.VMEM((2, BLK, BLK), jnp.bfloat16),
            pltpu.VMEM((16, 16, BLK), jnp.bfloat16),
            pltpu.VMEM((2, 2, 8, BLK), f32),
            pltpu.VMEM((4, 2, 8, BLK), f32),
            pltpu.VMEM((1, 2, 8, BLK), f32),
            pltpu.VMEM((7, 2, 8, BLK), f32),
            pltpu.VMEM((7, 2, 8, BLK), f32),
            pltpu.VMEM((3, 2, 8, BLK), f32),
            pltpu.VMEM((2, 8, BLK), f32),
            dma((2,)),
            dma((4 * RAW + 1,)), dma((4 * RAW + 1,)),
            dma((2 * NSLOT,)), dma((2 * NSLOT,)),
            dma((2 * NSLOT,)), dma((2 * NSLOT,)),
            dma((19,)), dma((19,)),
            dma((16,)), dma((16,)),
        ],
        compiler_params=pltpu.CompilerParams(
            collective_id=0, has_side_effects=True,
            vmem_limit_bytes=48 * 1024 * 1024),
        name="kfac",
    )(pltpu.with_memory_space_constraint(act_input, pltpu.HBM),
      pltpu.with_memory_space_constraint(out_grad, pltpu.HBM))
    return act_out[None, None], grad_out[None, None]


def solution(mesh):
    placed = (P(("dp", "ctx"), None), P(("dp", "ctx"), None))
    return jax.shard_map(
        on_device,
        mesh=mesh,
        in_specs=placed,
        out_specs=(P("ctx", "dp", None, None), P("ctx", "dp", None, None)),
        check_vma=False,
    )
```

```python
import jax
import jax.numpy as jnp
from jax import lax
from jax.experimental import pallas as pl
from jax.experimental.pallas import tpu as pltpu
from jax.sharding import PartitionSpec as P

damping = 1.0

NX, NY, NZ = 4, 8, 8
ROWS = 160
HALF = ROWS // 2
W = 2048
HW = W // 2
BLK = 128
NB = HW // BLK
TOKENS = ROWS * 2 * NX * NY * NZ
MESH = pl.DeviceIdType.MESH

STREAMS = ((0, 1, 4), (1, -1, 4), (2, 1, 4), (3, -1, 4),
           (1, 1, 3), (0, -1, 3), (3, 1, 3), (2, -1, 3))
BASE = (0, 4, 8, 12, 16, 19, 22, 25)
NSLOT = 28
RAW = 4
CHUNK = 128
CODE_TOP = 2.0 ** 15


def device(x, y, z, c):
    return (x * (NZ // 2) + z // 2, (z % 2) * (2 * NY) + y * 2 + c)


def kernel(act, grad, act_out, grad_out,
           xb, ob, pk, q1, r1, q2, r2, outbox, inbox, dl, dg, gd, gy, gz, gx, gc,
           near, loc_sem, raw_s, raw_r, s1_s, s1_r, s2_s, s2_r,
           dg_s, dg_r, out_s, out_r):
    dp = lax.axis_index("dp")
    ctx = lax.axis_index("ctx")
    x = dp // (NZ // 2)
    z = (dp % (NZ // 2)) * 2 + ctx // (2 * NY)
    y = (ctx // 2) % NY
    c = ctx % 2
    par = x % 2

    def at_x(d):
        return device((x + d) % NX, y, z, c)

    def at_y(d):
        return device(x, (y + d) % NY, z, c)

    def at_z(d):
        return device(x, y, (z + d) % NZ, c)

    partner = device(x, y, z, 1 - c)

    def remote(src, dst, ssem, rsem, dev):
        return pltpu.make_async_remote_copy(
            src_ref=src, dst_ref=dst, send_sem=ssem, recv_sem=rsem,
            device_id=dev, device_id_type=MESH)

    barrier = pltpu.get_barrier_semaphore()
    around = [at_y(1), at_y(-1), at_z(1), at_z(-1)]
    peers = [partner, at_x(1), at_x(-1)] + around
    for dev in peers:
        pl.semaphore_signal(barrier, inc=1, device_id=dev, device_id_type=MESH)

    own_rows = xb.at[pl.ds(0, ROWS)]

    @pl.when(par == 0)
    def _():
        pltpu.make_async_copy(act, own_rows, loc_sem.at[0]).start()
        pltpu.make_async_copy(grad, ob, loc_sem.at[1]).start()

    @pl.when(par == 1)
    def _():
        pltpu.make_async_copy(grad, own_rows, loc_sem.at[0]).start()
        pltpu.make_async_copy(act, ob, loc_sem.at[1]).start()

    pl.semaphore_wait(barrier, len(peers))

    def raw_copies(own, other):
        copies = []
        for h in range(RAW):
            cols = pl.ds(h * (W // RAW), W // RAW)
            copies.append(remote(
                other.at[pl.ds(0, HALF), cols],
                xb.at[pl.ds(2 * ROWS, HALF), cols],
                raw_s.at[2 * h], raw_r.at[2 * h], at_x(1)))
            copies.append(remote(
                other.at[pl.ds(HALF, HALF), cols],
                xb.at[pl.ds(2 * ROWS + HALF, HALF), cols],
                raw_s.at[2 * h + 1], raw_r.at[2 * h + 1], at_x(-1)))
        copies.append(remote(own, xb.at[pl.ds(ROWS, ROWS)],
                             raw_s.at[2 * RAW], raw_r.at[2 * RAW], partner))
        return copies

    @pl.when(par == 0)
    def _():
        for copy in raw_copies(act, grad):
            copy.start()

    @pl.when(par == 1)
    def _():
        for copy in raw_copies(grad, act):
            copy.start()

    def tell(n):
        for dev in around:
            pl.semaphore_signal(near.at[n], inc=1, device_id=dev, device_id_type=MESH)

    def hear(n):
        pl.semaphore_wait(near.at[n], len(around))

    tell(0)
    raw = raw_copies(act, grad)
    pltpu.make_async_copy(act, own_rows, loc_sem.at[0]).wait()
    pltpu.make_async_copy(act, ob, loc_sem.at[1]).wait()

    diag_copies = []

    def diag_send(srcs, dsts, devs, base):
        copies = []
        for n, (src, dst, dev) in enumerate(zip(srcs, dsts, devs)):
            copy = remote(src, dst, dg_s.at[base + n], dg_r.at[base + n], dev)
            copy.start()
            copies.append(copy)
        diag_copies.extend(copies)
        return copies

    def diag_sum(first, copies, slots, to):
        total = dg[first]
        for n, copy in enumerate(copies):
            copy.wait_recv()
            total = total + slots[n]
        dg[to] = total

    for tokens, f in ((own_rows, par), (ob, 1 - par)):
        for i in range(2 * NB):
            part = tokens[:, BLK * i:BLK * (i + 1)].astype(jnp.float32)
            dl[i // NB, f, pl.ds(i % NB, 1), :] = jnp.sum(part * part, axis=0, keepdims=True)
    pending = {"d": diag_send([dl.at[1 - c]], [gd.at[0]], [partner], 0)}
    hear(0)
    tell(1)
    raw[2 * RAW].wait_recv()

    contract = (((0,), (0,)), ((), ()))

    def product(rows, left, right):
        return lax.dot_general(xb[rows, left], xb[rows, right], contract,
                               preferred_element_type=jnp.float32)

    upper = (lax.broadcasted_iota(jnp.int32, (256, 256), 0)
             < lax.broadcasted_iota(jnp.int32, (256, 256), 1))

    def store(a, b, value, add):
        for i in range(2):
            for j in range(2):
                part = value[BLK * i:BLK * (i + 1), BLK * j:BLK * (j + 1)]
                if add:
                    part = part + pk[2 * a + i, 2 * b + j]
                pk[2 * a + i, 2 * b + j] = part

    def tile_grid(row, add):
        rows = pl.ds(row, 2 * ROWS)

        @pl.when(c == 0)
        def _():
            for a in range(4):
                value = product(rows, pl.ds(256 * a, 256), pl.ds(HW, HW))
                for b in range(4):
                    store(a, b, value[:, 256 * b:256 * (b + 1)], add)

        @pl.when(c == 1)
        def _():
            for a in range(4):
                first = product(rows, pl.ds(256 * a, 256), pl.ds(256 * a, HW - 256 * a))
                second = product(rows, pl.ds(HW + 256 * a, 256), pl.ds(HW, 256 * (a + 1)))
                for b in range(4):
                    high = first[:, 256 * (b - a):256 * (b - a + 1)] if b >= a else None
                    low = second[:, 256 * b:256 * (b + 1)] if b <= a else None
                    if high is None:
                        store(a, b, low, add)
                    elif low is None:
                        store(a, b, high, add)
                    else:
                        store(a, b, jnp.where(upper, high, low), add)

    hear(1)
    tell(2)
    tile_grid(0, False)

    dg[0] = dl[c]
    diag_sum(0, pending["d"], gd, 0)
    hear(2)
    pending["y"] = diag_send([dg.at[0]] * 7, [gy.at[d - 1] for d in range(1, NY)],
                             [at_y(d) for d in range(1, NY)], 1)

    relay = []
    for h in range(RAW):
        for s in range(2):
            raw[2 * h + s].wait_recv()
            rows = pl.ds(2 * ROWS + HALF * s, HALF)
            to = pl.ds(3 * ROWS + HALF * s, HALF)
            cols = pl.ds(h * (W // RAW), W // RAW)
            slot = 2 * RAW + 1 + 2 * h + s
            copy = remote(xb.at[rows, cols], xb.at[to, cols],
                          raw_s.at[slot], raw_r.at[slot], partner)
            copy.start()
            relay.append(copy)
    diag_sum(0, pending["y"], gy, 1)
    pending["z"] = diag_send([dg.at[1]] * 7, [gz.at[d - 1] for d in range(1, NZ)],
                             [at_z(d) for d in range(1, NZ)], 8)
    for copy in relay:
        copy.wait_recv()

    tile_grid(2 * ROWS, True)

    def chunk1(k, o, h):
        if k == 0:
            return pk.at[o, pl.ds(2 * h, 2), pl.ds(0, 64), :]
        return pk.at[pl.ds(2 * h, 2), o, pl.ds(64, 64), :]

    def power(v):
        for _ in range(3):
            v = v * jnp.abs(v)
        return v

    def root(y):
        r = lax.rsqrt(lax.rsqrt(jnp.maximum(jnp.abs(y), 1.2e-38)))
        r = r * lax.rsqrt(r)
        return jnp.where(y < 0, -r, r)

    def encode(value, ref):
        n = value.shape[0]
        tiles = value.reshape(n // 8, 8, BLK)
        top = jnp.max(jnp.abs(tiles), axis=0)
        scale = (CODE_TOP / jnp.maximum(top, 1e-30)).astype(jnp.bfloat16)
        y = power(tiles * scale.astype(jnp.float32)[None])
        ref[pl.ds(0, n), :] = y.reshape(n, BLK).astype(jnp.bfloat16)
        ref[pl.ds(n, 16), :] = jnp.concatenate([scale, scale], axis=0)

    def decode(ref, n):
        y = ref[pl.ds(0, n), :].astype(jnp.float32).reshape(n // 8, 8, BLK)
        inverse = 1.0 / ref[pl.ds(n, 16), :].astype(jnp.float32)[0:8]
        return (root(y) * inverse[None]).reshape(n, BLK)

    def ring(chunk, sent, slots, ssem, rsem, axes, between):
        copies = {}
        for t in range(5):
            for i, (h, sign, hops) in enumerate(STREAMS):
                if t > hops:
                    continue
                for k in range(2):
                    pos, at = axes[k]
                    o = (pos + sign * (hops - t)) % NY
                    ref = chunk(k, o, h)
                    value = ref[...].reshape(CHUNK, BLK)
                    if t > 0:
                        copies[k, i, t - 1].wait_recv()
                        value = value + decode(slots.at[k * NSLOT + BASE[i] + t - 1], CHUNK)
                    if t == hops:
                        ref[...] = value.reshape(2, 64, BLK)
                    else:
                        slot = k * NSLOT + BASE[i] + t
                        encode(value, sent.at[slot])
                        copy = remote(sent.at[slot], slots.at[slot], ssem.at[slot],
                                      rsem.at[slot], at(sign))
                        copy.start()
                        copies[k, i, t] = copy
            between(t)
        return copies

    def between1(t):
        if t == 1:
            diag_sum(1, pending["z"], gz, 2)
            pending["x"] = diag_send([dg.at[2]] * 3, [gx.at[d - 1] for d in range(1, NX)],
                                     [at_x(d) for d in range(1, NX)], 15)
        elif t == 2:
            diag_sum(2, pending["x"], gx, 3)
            pending["c"] = diag_send([dg.at[3]], [gc], [partner], 18)
        elif t == 3:
            pending["c"][0].wait_recv()

    first = ring(chunk1, q1, r1, s1_s, s1_r, ((y, at_y), (z, at_z)), between1)
    row_block = (z % 2) * 8 + (y % 2) * 4 + c * 2 + x // 2
    strip = (x % 2) * 4 + z // 2
    own_half = (row_block // 8) == c
    pick = lax.broadcasted_iota(jnp.int32, (8, BLK), 0) == row_block % 8
    trace = []
    values = []
    for f in range(2):
        a, b = dg[3, f], gc[f]
        trace.append(jnp.sum(a + b, keepdims=True))
        chosen = jnp.where(own_half, a, b)
        values.append(jnp.sum(jnp.where(pick, chosen, 0.0), axis=0, keepdims=True))
    bound = [jnp.maximum(t, 1e-30) for t in trace]
    my_bound = jnp.where(par == 0, bound[0], bound[1])
    to_code = CODE_TOP / my_bound
    from_code = my_bound / CODE_TOP

    second = []
    for d in (4, 3, 5, 2, 6, 1, 7):
        for k in range(2):
            if k == 0:
                value, dev = pk[y, (z + d) % NZ, pl.ds(0, 64), :], at_z(d)
            else:
                value, dev = pk[(y + d) % NY, z, pl.ds(64, 64), :], at_y(d)
            slot = 7 * k + d - 1
            q2[slot] = power(value * to_code).astype(jnp.bfloat16)
            copy = remote(q2.at[slot], r2.at[slot], s2_s.at[slot], s2_r.at[slot], dev)
            copy.start()
            second.append((k, slot, copy))
    sums = [pk[y, z, pl.ds(0, 64), :], pk[y, z, pl.ds(64, 64), :]]
    for k, slot, copy in sorted(second, key=lambda e: min(e[1] % 7, 6 - e[1] % 7)):
        copy.wait_recv()
        sums[k] = sums[k] + root(r2[slot].astype(jnp.float32)) * from_code

    piece = power(jnp.concatenate(sums, axis=0) * to_code)
    flipped = piece.T
    below = (lax.broadcasted_iota(jnp.int32, (BLK, BLK), 0)
             > lax.broadcasted_iota(jnp.int32, (BLK, BLK), 1))
    packed = jnp.logical_and(c == 1, y == z)
    swap = jnp.logical_and(below, packed)
    outbox[0] = jnp.where(swap, flipped, piece).astype(jnp.bfloat16)
    outbox[1] = jnp.where(swap, piece, flipped).astype(jnp.bfloat16)

    off_a = jnp.where(y > z, NB, 0)
    off_b = jnp.where(y >= z, NB, 0)
    blocks = (
        (y + jnp.where(c == 0, 0, off_a), z + jnp.where(c == 0, NB, off_a)),
        (z + jnp.where(c == 0, NB, off_b), y + jnp.where(c == 0, 0, off_b)),
    )
    me = (dp, ctx)
    sends = []
    for g in range(2):
        bi, bj = blocks[g]
        slot = par * 8 + (x // 2) * 4 + bj % 4
        for s in range(8):
            dev = device(2 * (bi % 2) + s // 4, 2 * (bj // 4) + (bi // 4) % 2,
                         2 * (s % 4) + bi // 8, (bi // 2) % 2)
            is_me = jnp.logical_and(dev[0] == me[0], dev[1] == me[1])
            src = outbox.at[g, pl.ds(16 * s, 16), :]
            dst = inbox.at[slot]
            copy = remote(src, dst, out_s.at[8 * g + s], out_r.at[slot], dev)

            @pl.when(is_me)
            def _():
                pltpu.make_async_copy(src, dst, out_r.at[slot]).start()

            @pl.when(jnp.logical_not(is_me))
            def _():
                copy.start()
            sends.append((copy, is_me))

    ratio = jnp.sqrt(trace[0] / trace[1])
    shift = (ratio * damping, damping / ratio)
    scale = 1.0 / TOKENS
    on_diag = (lax.broadcasted_iota(jnp.int32, (16, BLK), 1)
               == lax.broadcasted_iota(jnp.int32, (16, BLK), 0) + 16 * strip)
    for f in range(2):
        out = (act_out, grad_out)[f]
        damped = values[f] * scale + shift[f]
        for j in range(4):
            for n in range(2):
                slot = 8 * f + 4 * n + j
                pltpu.make_async_copy(outbox.at[0, pl.ds(0, 16), :], inbox.at[slot],
                                      out_r.at[slot]).wait()
            here = jnp.logical_and(on_diag, (y // 2) * 4 + j == row_block)
            value = (root(inbox[8 * f + j].astype(jnp.float32))
                     + root(inbox[8 * f + 4 + j].astype(jnp.float32)))
            value = value * (bound[f] * (scale / CODE_TOP))
            out[:, BLK * j:BLK * (j + 1)] = jnp.where(here, damped, value)

    for copy, is_me in sends:
        @pl.when(jnp.logical_not(is_me))
        def _():
            copy.wait_send()
    for copy in raw + relay + list(first.values()) + [copy for _, _, copy in second] + diag_copies:
        copy.wait_send()


def on_device(act_input, out_grad):
    f32 = jnp.float32
    piece = jax.ShapeDtypeStruct((16, 4 * BLK), f32)
    any_space = pl.BlockSpec(memory_space=pltpu.HBM)
    vmem = pl.BlockSpec(memory_space=pltpu.VMEM)
    dma = pltpu.SemaphoreType.DMA
    act_out, grad_out = pl.pallas_call(
        kernel,
        out_shape=(piece, piece),
        in_specs=[any_space, any_space],
        out_specs=(vmem, vmem),
        scratch_shapes=[
            pltpu.VMEM((4 * ROWS, W), jnp.bfloat16),
            pltpu.VMEM((ROWS, W), jnp.bfloat16),
            pltpu.VMEM((NB, NB, BLK, BLK), f32),
            pltpu.VMEM((2 * NSLOT, CHUNK + 16, BLK), jnp.bfloat16),
            pltpu.VMEM((2 * NSLOT, CHUNK + 16, BLK), jnp.bfloat16),
            pltpu.VMEM((14, 64, BLK), jnp.bfloat16),
            pltpu.VMEM((14, 64, BLK), jnp.bfloat16),
            pltpu.VMEM((2, BLK, BLK), jnp.bfloat16),
            pltpu.VMEM((16, 16, BLK), jnp.bfloat16),
            pltpu.VMEM((2, 2, 8, BLK), f32),
            pltpu.VMEM((4, 2, 8, BLK), f32),
            pltpu.VMEM((1, 2, 8, BLK), f32),
            pltpu.VMEM((7, 2, 8, BLK), f32),
            pltpu.VMEM((7, 2, 8, BLK), f32),
            pltpu.VMEM((3, 2, 8, BLK), f32),
            pltpu.VMEM((2, 8, BLK), f32),
            pltpu.SemaphoreType.REGULAR((3,)),
            dma((2,)),
            dma((4 * RAW + 1,)), dma((4 * RAW + 1,)),
            dma((2 * NSLOT,)), dma((2 * NSLOT,)),
            dma((2 * NSLOT,)), dma((2 * NSLOT,)),
            dma((19,)), dma((19,)),
            dma((16,)), dma((16,)),
        ],
        compiler_params=pltpu.CompilerParams(
            collective_id=0, has_side_effects=True,
            vmem_limit_bytes=48 * 1024 * 1024),
        name="kfac",
    )(pltpu.with_memory_space_constraint(act_input, pltpu.HBM),
      pltpu.with_memory_space_constraint(out_grad, pltpu.HBM))
    return act_out[None, None], grad_out[None, None]


def solution(mesh):
    placed = (P(("dp", "ctx"), None), P(("dp", "ctx"), None))
    return jax.shard_map(
        on_device,
        mesh=mesh,
        in_specs=placed,
        out_specs=(P("ctx", "dp", None, None), P("ctx", "dp", None, None)),
        check_vma=False,
    )
```

```python
import jax
import jax.numpy as jnp
from jax import lax
from jax.experimental import pallas as pl
from jax.experimental.pallas import tpu as pltpu
from jax.sharding import PartitionSpec as P

damping = 1.0

NX, NY, NZ = 4, 8, 8
ROWS = 160
HALF = ROWS // 2
W = 2048
HW = W // 2
BLK = 128
NB = HW // BLK
TOKENS = ROWS * 2 * NX * NY * NZ
MESH = pl.DeviceIdType.MESH

STREAMS = ((0, 1, 4), (1, -1, 4), (2, 1, 4), (3, -1, 4),
           (1, 1, 3), (0, -1, 3), (3, 1, 3), (2, -1, 3))
BASE = (0, 4, 8, 12, 16, 19, 22, 25)
NSLOT = 28
RAW = 4
CHUNK = 128
CODE_TOP = 2.0 ** 15


def device(x, y, z, c):
    return (x * (NZ // 2) + z // 2, (z % 2) * (2 * NY) + y * 2 + c)


def kernel(act, grad, outs,
           xb, ob, pk, q1, r1, q2, r2, outbox, inbox, dl, dg, gd, gy, gz, gx, gc,
           near, loc_sem, raw_s, raw_r, s1_s, s1_r, s2_s, s2_r,
           dg_s, dg_r, out_s, out_r):
    dp = lax.axis_index("dp")
    ctx = lax.axis_index("ctx")
    x = dp // (NZ // 2)
    z = (dp % (NZ // 2)) * 2 + ctx // (2 * NY)
    y = (ctx // 2) % NY
    c = ctx % 2
    par = x % 2

    def at_x(d):
        return device((x + d) % NX, y, z, c)

    def at_y(d):
        return device(x, (y + d) % NY, z, c)

    def at_z(d):
        return device(x, y, (z + d) % NZ, c)

    partner = device(x, y, z, 1 - c)

    def remote(src, dst, ssem, rsem, dev):
        return pltpu.make_async_remote_copy(
            src_ref=src, dst_ref=dst, send_sem=ssem, recv_sem=rsem,
            device_id=dev, device_id_type=MESH)

    barrier = pltpu.get_barrier_semaphore()
    around = [at_y(1), at_y(-1), at_z(1), at_z(-1)]
    peers = [partner, at_x(1), at_x(-1)] + around
    for dev in peers:
        pl.semaphore_signal(barrier, inc=1, device_id=dev, device_id_type=MESH)

    own_rows = xb.at[pl.ds(0, ROWS)]

    @pl.when(par == 0)
    def _():
        pltpu.make_async_copy(act, own_rows, loc_sem.at[0]).start()
        pltpu.make_async_copy(grad, ob, loc_sem.at[1]).start()

    @pl.when(par == 1)
    def _():
        pltpu.make_async_copy(grad, own_rows, loc_sem.at[0]).start()
        pltpu.make_async_copy(act, ob, loc_sem.at[1]).start()

    pl.semaphore_wait(barrier, len(peers))

    def raw_copies(own, other):
        copies = []
        for h in range(RAW):
            cols = pl.ds(h * (W // RAW), W // RAW)
            copies.append(remote(
                other.at[pl.ds(0, HALF), cols],
                xb.at[pl.ds(2 * ROWS, HALF), cols],
                raw_s.at[2 * h], raw_r.at[2 * h], at_x(1)))
            copies.append(remote(
                other.at[pl.ds(HALF, HALF), cols],
                xb.at[pl.ds(2 * ROWS + HALF, HALF), cols],
                raw_s.at[2 * h + 1], raw_r.at[2 * h + 1], at_x(-1)))
        copies.append(remote(own, xb.at[pl.ds(ROWS, ROWS)],
                             raw_s.at[2 * RAW], raw_r.at[2 * RAW], partner))
        return copies

    @pl.when(par == 0)
    def _():
        for copy in raw_copies(act, grad):
            copy.start()

    @pl.when(par == 1)
    def _():
        for copy in raw_copies(grad, act):
            copy.start()

    def tell(n):
        for dev in around:
            pl.semaphore_signal(near.at[n], inc=1, device_id=dev, device_id_type=MESH)

    def hear(n):
        pl.semaphore_wait(near.at[n], len(around))

    tell(0)
    raw = raw_copies(act, grad)
    pltpu.make_async_copy(act, own_rows, loc_sem.at[0]).wait()
    pltpu.make_async_copy(act, ob, loc_sem.at[1]).wait()

    diag_copies = []

    def diag_send(srcs, dsts, devs, base):
        copies = []
        for n, (src, dst, dev) in enumerate(zip(srcs, dsts, devs)):
            copy = remote(src, dst, dg_s.at[base + n], dg_r.at[base + n], dev)
            copy.start()
            copies.append(copy)
        diag_copies.extend(copies)
        return copies

    def diag_sum(first, copies, slots, to):
        total = dg[first]
        for n, copy in enumerate(copies):
            copy.wait_recv()
            total = total + slots[n]
        dg[to] = total

    for tokens, f in ((own_rows, par), (ob, 1 - par)):
        for i in range(2 * NB):
            part = tokens[:, BLK * i:BLK * (i + 1)].astype(jnp.float32)
            dl[i // NB, f, pl.ds(i % NB, 1), :] = jnp.sum(part * part, axis=0, keepdims=True)
    pending = {"d": diag_send([dl.at[1 - c]], [gd.at[0]], [partner], 0)}
    hear(0)
    tell(1)
    raw[2 * RAW].wait_recv()

    contract = (((0,), (0,)), ((), ()))

    def product(rows, left, right):
        return lax.dot_general(xb[rows, left], xb[rows, right], contract,
                               preferred_element_type=jnp.float32)

    upper = (lax.broadcasted_iota(jnp.int32, (256, 256), 0)
             < lax.broadcasted_iota(jnp.int32, (256, 256), 1))

    def store(a, b, value, add):
        for i in range(2):
            for j in range(2):
                part = value[BLK * i:BLK * (i + 1), BLK * j:BLK * (j + 1)]
                if add:
                    part = part + pk[2 * a + i, 2 * b + j]
                pk[2 * a + i, 2 * b + j] = part

    def tile_grid(row, add):
        rows = pl.ds(row, 2 * ROWS)

        @pl.when(c == 0)
        def _():
            for a in range(4):
                value = product(rows, pl.ds(256 * a, 256), pl.ds(HW, HW))
                for b in range(4):
                    store(a, b, value[:, 256 * b:256 * (b + 1)], add)

        @pl.when(c == 1)
        def _():
            for a in range(4):
                first = product(rows, pl.ds(256 * a, 256), pl.ds(256 * a, HW - 256 * a))
                second = product(rows, pl.ds(HW + 256 * a, 256), pl.ds(HW, 256 * (a + 1)))
                for b in range(4):
                    high = first[:, 256 * (b - a):256 * (b - a + 1)] if b >= a else None
                    low = second[:, 256 * b:256 * (b + 1)] if b <= a else None
                    if high is None:
                        store(a, b, low, add)
                    elif low is None:
                        store(a, b, high, add)
                    else:
                        store(a, b, jnp.where(upper, high, low), add)

    hear(1)
    tell(2)
    tile_grid(0, False)

    dg[0] = dl[c]
    diag_sum(0, pending["d"], gd, 0)
    hear(2)
    pending["y"] = diag_send([dg.at[0]] * 7, [gy.at[d - 1] for d in range(1, NY)],
                             [at_y(d) for d in range(1, NY)], 1)

    relay = []
    for h in range(RAW):
        for s in range(2):
            raw[2 * h + s].wait_recv()
            rows = pl.ds(2 * ROWS + HALF * s, HALF)
            to = pl.ds(3 * ROWS + HALF * s, HALF)
            cols = pl.ds(h * (W // RAW), W // RAW)
            slot = 2 * RAW + 1 + 2 * h + s
            copy = remote(xb.at[rows, cols], xb.at[to, cols],
                          raw_s.at[slot], raw_r.at[slot], partner)
            copy.start()
            relay.append(copy)
    diag_sum(0, pending["y"], gy, 1)
    pending["z"] = diag_send([dg.at[1]] * 7, [gz.at[d - 1] for d in range(1, NZ)],
                             [at_z(d) for d in range(1, NZ)], 8)
    for copy in relay:
        copy.wait_recv()

    tile_grid(2 * ROWS, True)

    def chunk1(k, o, h):
        if k == 0:
            return pk.at[o, pl.ds(2 * h, 2), pl.ds(0, 64), :]
        return pk.at[pl.ds(2 * h, 2), o, pl.ds(64, 64), :]

    def power(v):
        for _ in range(3):
            v = v * jnp.abs(v)
        return v

    def root(y):
        r = lax.rsqrt(lax.rsqrt(jnp.maximum(jnp.abs(y), 1.2e-38)))
        r = r * lax.rsqrt(r)
        return jnp.where(y < 0, -r, r)

    def encode(value, ref):
        n = value.shape[0]
        tiles = value.reshape(n // 8, 8, BLK)
        top = jnp.max(jnp.abs(tiles), axis=0)
        scale = (CODE_TOP / jnp.maximum(top, 1e-30)).astype(jnp.bfloat16)
        y = power(tiles * scale.astype(jnp.float32)[None])
        ref[pl.ds(0, n), :] = y.reshape(n, BLK).astype(jnp.bfloat16)
        ref[pl.ds(n, 16), :] = jnp.concatenate([scale, scale], axis=0)

    def decode(ref, n):
        y = ref[pl.ds(0, n), :].astype(jnp.float32).reshape(n // 8, 8, BLK)
        inverse = 1.0 / ref[pl.ds(n, 16), :].astype(jnp.float32)[0:8]
        return (root(y) * inverse[None]).reshape(n, BLK)

    def ring(chunk, sent, slots, ssem, rsem, axes, between):
        copies = {}
        for t in range(5):
            for i, (h, sign, hops) in enumerate(STREAMS):
                if t > hops:
                    continue
                for k in range(2):
                    pos, at = axes[k]
                    o = (pos + sign * (hops - t)) % NY
                    ref = chunk(k, o, h)
                    value = ref[...].reshape(CHUNK, BLK)
                    if t > 0:
                        copies[k, i, t - 1].wait_recv()
                        value = value + decode(slots.at[k * NSLOT + BASE[i] + t - 1], CHUNK)
                    if t == hops:
                        ref[...] = value.reshape(2, 64, BLK)
                    else:
                        slot = k * NSLOT + BASE[i] + t
                        encode(value, sent.at[slot])
                        copy = remote(sent.at[slot], slots.at[slot], ssem.at[slot],
                                      rsem.at[slot], at(sign))
                        copy.start()
                        copies[k, i, t] = copy
            between(t)
        return copies

    def between1(t):
        if t == 1:
            diag_sum(1, pending["z"], gz, 2)
            pending["x"] = diag_send([dg.at[2]] * 3, [gx.at[d - 1] for d in range(1, NX)],
                                     [at_x(d) for d in range(1, NX)], 15)
        elif t == 2:
            diag_sum(2, pending["x"], gx, 3)
            pending["c"] = diag_send([dg.at[3]], [gc], [partner], 18)
        elif t == 3:
            pending["c"][0].wait_recv()

    first = ring(chunk1, q1, r1, s1_s, s1_r, ((y, at_y), (z, at_z)), between1)
    row_block = (z % 2) * 8 + (y % 2) * 4 + c * 2 + x // 2
    strip = (x % 2) * 4 + z // 2
    own_half = (row_block // 8) == c
    pick = lax.broadcasted_iota(jnp.int32, (8, BLK), 0) == row_block % 8
    trace = []
    values = []
    for f in range(2):
        a, b = dg[3, f], gc[f]
        trace.append(jnp.sum(a + b, keepdims=True))
        chosen = jnp.where(own_half, a, b)
        values.append(jnp.sum(jnp.where(pick, chosen, 0.0), axis=0, keepdims=True))
    bound = [jnp.maximum(t, 1e-30) for t in trace]
    my_bound = jnp.where(par == 0, bound[0], bound[1])
    to_code = CODE_TOP / my_bound
    from_code = my_bound / CODE_TOP

    second = []
    for d in (4, 3, 5, 2, 6, 1, 7):
        for k in range(2):
            if k == 0:
                value, dev = pk[y, (z + d) % NZ, pl.ds(0, 64), :], at_z(d)
            else:
                value, dev = pk[(y + d) % NY, z, pl.ds(64, 64), :], at_y(d)
            slot = 7 * k + d - 1
            q2[slot] = power(value * to_code).astype(jnp.bfloat16)
            copy = remote(q2.at[slot], r2.at[slot], s2_s.at[slot], s2_r.at[slot], dev)
            copy.start()
            second.append((k, slot, copy))
    sums = [pk[y, z, pl.ds(0, 64), :], pk[y, z, pl.ds(64, 64), :]]
    for k, slot, copy in sorted(second, key=lambda e: min(e[1] % 7, 6 - e[1] % 7)):
        copy.wait_recv()
        sums[k] = sums[k] + root(r2[slot].astype(jnp.float32)) * from_code

    piece = power(jnp.concatenate(sums, axis=0) * to_code)
    flipped = piece.T
    below = (lax.broadcasted_iota(jnp.int32, (BLK, BLK), 0)
             > lax.broadcasted_iota(jnp.int32, (BLK, BLK), 1))
    packed = jnp.logical_and(c == 1, y == z)
    swap = jnp.logical_and(below, packed)
    outbox[0] = jnp.where(swap, flipped, piece).astype(jnp.bfloat16)
    outbox[1] = jnp.where(swap, piece, flipped).astype(jnp.bfloat16)

    off_a = jnp.where(y > z, NB, 0)
    off_b = jnp.where(y >= z, NB, 0)
    blocks = (
        (y + jnp.where(c == 0, 0, off_a), z + jnp.where(c == 0, NB, off_a)),
        (z + jnp.where(c == 0, NB, off_b), y + jnp.where(c == 0, 0, off_b)),
    )
    me = (dp, ctx)
    sends = []
    for g in range(2):
        bi, bj = blocks[g]
        slot = par * 8 + (x // 2) * 4 + bj % 4
        for s in range(8):
            dev = device(2 * (bi % 2) + s // 4, 2 * (bj // 4) + (bi // 4) % 2,
                         2 * (s % 4) + bi // 8, (bi // 2) % 2)
            is_me = jnp.logical_and(dev[0] == me[0], dev[1] == me[1])
            src = outbox.at[g, pl.ds(16 * s, 16), :]
            dst = inbox.at[slot]
            copy = remote(src, dst, out_s.at[8 * g + s], out_r.at[slot], dev)

            @pl.when(is_me)
            def _():
                pltpu.make_async_copy(src, dst, out_r.at[slot]).start()

            @pl.when(jnp.logical_not(is_me))
            def _():
                copy.start()
            sends.append((copy, is_me))

    ratio = jnp.sqrt(trace[0] / trace[1])
    shift = (ratio * damping, damping / ratio)
    scale = 1.0 / TOKENS
    on_diag = (lax.broadcasted_iota(jnp.int32, (16, BLK), 1)
               == lax.broadcasted_iota(jnp.int32, (16, BLK), 0) + 16 * strip)
    for f in range(2):
        damped = values[f] * scale + shift[f]
        for j in range(4):
            for n in range(2):
                slot = 8 * f + 4 * n + j
                pltpu.make_async_copy(outbox.at[0, pl.ds(0, 16), :], inbox.at[slot],
                                      out_r.at[slot]).wait()
            here = jnp.logical_and(on_diag, (y // 2) * 4 + j == row_block)
            value = (root(inbox[8 * f + j].astype(jnp.float32))
                     + root(inbox[8 * f + 4 + j].astype(jnp.float32)))
            value = value * (bound[f] * (scale / CODE_TOP))
            outs[f, :, BLK * j:BLK * (j + 1)] = jnp.where(here, damped, value)

    for copy, is_me in sends:
        @pl.when(jnp.logical_not(is_me))
        def _():
            copy.wait_send()
    for copy in raw + relay + list(first.values()) + [copy for _, _, copy in second] + diag_copies:
        copy.wait_send()


def on_device(act_input, out_grad):
    f32 = jnp.float32
    piece = jax.ShapeDtypeStruct((2, 16, 4 * BLK), f32)
    any_space = pl.BlockSpec(memory_space=pltpu.HBM)
    vmem = pl.BlockSpec(memory_space=pltpu.VMEM)
    dma = pltpu.SemaphoreType.DMA
    outs = pl.pallas_call(
        kernel,
        out_shape=piece,
        in_specs=[any_space, any_space],
        out_specs=vmem,
        scratch_shapes=[
            pltpu.VMEM((4 * ROWS, W), jnp.bfloat16),
            pltpu.VMEM((ROWS, W), jnp.bfloat16),
            pltpu.VMEM((NB, NB, BLK, BLK), f32),
            pltpu.VMEM((2 * NSLOT, CHUNK + 16, BLK), jnp.bfloat16),
            pltpu.VMEM((2 * NSLOT, CHUNK + 16, BLK), jnp.bfloat16),
            pltpu.VMEM((14, 64, BLK), jnp.bfloat16),
            pltpu.VMEM((14, 64, BLK), jnp.bfloat16),
            pltpu.VMEM((2, BLK, BLK), jnp.bfloat16),
            pltpu.VMEM((16, 16, BLK), jnp.bfloat16),
            pltpu.VMEM((2, 2, 8, BLK), f32),
            pltpu.VMEM((4, 2, 8, BLK), f32),
            pltpu.VMEM((1, 2, 8, BLK), f32),
            pltpu.VMEM((7, 2, 8, BLK), f32),
            pltpu.VMEM((7, 2, 8, BLK), f32),
            pltpu.VMEM((3, 2, 8, BLK), f32),
            pltpu.VMEM((2, 8, BLK), f32),
            pltpu.SemaphoreType.REGULAR((3,)),
            dma((2,)),
            dma((4 * RAW + 1,)), dma((4 * RAW + 1,)),
            dma((2 * NSLOT,)), dma((2 * NSLOT,)),
            dma((2 * NSLOT,)), dma((2 * NSLOT,)),
            dma((19,)), dma((19,)),
            dma((16,)), dma((16,)),
        ],
        compiler_params=pltpu.CompilerParams(
            collective_id=0, has_side_effects=True,
            vmem_limit_bytes=48 * 1024 * 1024),
        name="kfac",
    )(pltpu.with_memory_space_constraint(act_input, pltpu.HBM),
      pltpu.with_memory_space_constraint(out_grad, pltpu.HBM))
    return outs[0][None, None], outs[1][None, None]


def solution(mesh):
    placed = (P(("dp", "ctx"), None), P(("dp", "ctx"), None))
    return jax.shard_map(
        on_device,
        mesh=mesh,
        in_specs=placed,
        out_specs=(P("ctx", "dp", None, None), P("ctx", "dp", None, None)),
        check_vma=False,
    )
```
